256 devices in a mesh: slab: 32 (over y, z), ray: 8 (over x, core).
Axes of the slice: x: 4, y: 4, z: 8, core: 2. Of those that a mesh axis runs over, the one named last changes fastest.
Arguments:
- ray_code: bfloat16 [4096, 128], P(('ray', 'slab')), may hold values from -4 to 4
- direction: int32 [4096], P('ray'), may hold values from 0 to 1
- target: float32 [3, 4096], P(None, 'ray'), may hold values from 0 to 1
- brick_code: bfloat16 [32, 1024, 128], P('slab'), may hold values from -4 to 4
- sample_code: bfloat16 [32, 64, 128], P('slab'), may hold values from -4 to 4
- w_hidden: bfloat16 [32, 128, 128], P('slab'), may hold values from -0.5 to 0.5
- b_hidden: float32 [32, 128], P('slab'), may hold values from -3 to 3
- w_out: bfloat16 [32, 4, 128], P('slab'), may hold values from -0.5 to 0.5
- b_out: float32 [32, 4], P('slab'), may hold values from -4 to 4
- brick_ids: int32 [32, 2, 4096], P('slab', None, 'ray'), may hold values from 0 to 1023
- occupancy: int32 [32, 4096], P('slab', 'ray'), may hold values from 0 to 2, as said below
Outputs:
- color: float32 [3, 4096], P(None, ('ray', 'slab'))
- grad_ray: float32 [4096, 128], P(('ray', 'slab'))
- grad_brick: float32 [32, 1024, 128], P('slab', 'ray')
- grad_sample: float32 [32, 64, 128], P('slab')
- grad_w_hidden: float32 [32, 128, 128], P('slab')
- grad_b_hidden: float32 [32, 128], P('slab')
- grad_w_out: float32 [32, 4, 128], P('slab')
- grad_b_out: float32 [32, 4], P('slab')
The draws below stay inside these ranges and needn't reach their ends.
Inputs may be any that keep to these rules, and one draw needn't show every extreme that they name: Slots k >= occupancy[s, r] are padding and carry no density; every slab has a ray segment with 2 occupied slots. `brick_ids`: padded slots still name some brick of the slab's table.
All inputs are finite; a program needn't handle non-finite values.
Results may differ from the reference program's by a relative error of at most 0.008.
Values may be sent and summed in bfloat16 or wider, within the bound.
A program may use at most 64 MiB of HBM per device.

```python
import math
import jax
import jax.numpy as jnp
import numpy as np
from jax import lax

D = 128
SAMPLES = 64
BMAX = 2
BRICKS = 1024
SLABS = 32
RAYS = 4096


def draw_occupancy(key, part):
    level_key, spread_key = jax.random.split(jax.random.fold_in(key, 17))
    slab_level = jax.random.randint(level_key, (SLABS, 1), 0, 4)
    spread = jax.random.randint(spread_key, (SLABS, RAYS), 0, 4)
    counted = jnp.clip(spread + slab_level - 2, 0, BMAX)
    first_ray = jnp.arange(RAYS)[None, :] == 0
    return jnp.where(first_ray, BMAX, counted).astype(jnp.int32)


def set_ends(values, own_key, least, top_value):
    shape = values.shape
    place = [jax.random.randint(jax.random.fold_in(own_key, axis), (), 0, shape[axis]) for axis in range(len(shape))]
    values = values.at[tuple(place)].set(least)
    longest = shape.index(max(shape))
    place[longest] = (place[longest] + 1) % shape[longest]
    return values.at[tuple(place)].set(top_value)


def shard_levels(key, dims, cuts, least, largest):
    factor_of, own = 1.0, jax.random.fold_in(key, 6)
    for dim, blocks in cuts:
        heights = jnp.exp(jax.random.uniform(jax.random.fold_in(own, dim), (blocks,), jnp.float32, least / len(cuts), largest / len(cuts)))
        factor_of = factor_of * jnp.repeat(heights, dims[dim] // blocks).reshape([-1 if axis == dim else 1 for axis in range(len(dims))])
    return factor_of


def rank_bounds(count, lean):
    weights = [(1 << 20) // math.isqrt(standing ** lean) + 1 for standing in range(1, count + 1)]
    deviation = 1 + sum(weights) // (1 << 30)
    return np.cumsum(np.array([max(1, weight // deviation) for weight in weights]))


def ranked(own_key, extent, count, lean):
    table = rank_bounds(count, lean)
    ticket = jax.random.randint(jax.random.fold_in(own_key, 1), extent, 0, int(table[count - 1]))
    rank = jnp.searchsorted(jnp.asarray(table, jnp.int32), ticket, side="right")
    return jax.random.permutation(jax.random.fold_in(own_key, 2), count)[rank].astype(jnp.int32)


def gaussian(key, shape, scale, bound, cuts=(), kind=jnp.bfloat16):
    entries = jax.random.normal(key, shape, jnp.float32) * scale
    if len(cuts) > 0:
        entries = shard_levels(key, shape, cuts, -0.22, 0.18) * entries
    return jnp.clip(entries, min=-bound, max=bound).astype(kind)


def setup_inputs(seed: int = 0) -> dict:
    arg_keys = jax.random.split(jax.random.key(seed), 12)
    return {
        "ray_code": gaussian(arg_keys[0], (RAYS, D), 0.6, 4.0, ((0, 256),)),
        "direction": set_ends(jax.random.randint(arg_keys[1], (RAYS,), 0, 2), jax.random.fold_in(arg_keys[1], 1), 0, 1).astype(jnp.int32),
        "target": jnp.clip(1.0 * jax.random.uniform(arg_keys[2], (3, RAYS), jnp.float32) ** shard_levels(arg_keys[2], (3, RAYS), ((1, 8),), -0.2, 0.2), 0.0, 1.0),
        "brick_code": gaussian(arg_keys[3], (SLABS, BRICKS, D), 0.6, 4.0, ((0, 32),)),
        "sample_code": gaussian(arg_keys[4], (SLABS, SAMPLES, D), 0.6, 4.0, ((0, 32),)),
        "w_hidden": gaussian(arg_keys[5], (SLABS, D, D), D ** -0.5, 0.5, ((0, 32),)),
        "b_hidden": gaussian(arg_keys[6], (SLABS, D), 0.5, 3.0, ((0, 32),), jnp.float32),
        "w_out": gaussian(arg_keys[7], (SLABS, 4, D), D ** -0.5, 0.5, ((0, 32),)),
        "b_out": gaussian(arg_keys[8], (SLABS, 4), 1.0, 4.0, ((0, 32),), jnp.float32),
        "brick_ids": set_ends(ranked(arg_keys[9], (SLABS, BMAX, RAYS), BRICKS, 2), jax.random.fold_in(arg_keys[9], 3), 0, BRICKS - 1).astype(jnp.int32),
        "occupancy": draw_occupancy(jax.random.fold_in(arg_keys[11], 71), 0),
    }


step_length = 0.002


def shade_forward(brick_rows, sample_rows, ray_rows, slot_ids, occupied_count, hidden_w, hidden_b, out_w, out_b):
    chosen = jnp.take(brick_rows, slot_ids.T, axis=0)
    summed = (chosen.astype(jnp.float32)[:, :, None, :] + sample_rows.astype(jnp.float32)[None, None, :, :]
              + ray_rows.astype(jnp.float32)[:, None, None, :])
    inputs = summed.astype(jnp.bfloat16).reshape(-1, summed.shape[-1])
    preact = jnp.dot(inputs, hidden_w, preferred_element_type=jnp.float32) + hidden_b[None, :]
    hidden = jnp.maximum(preact, 0.0).astype(jnp.bfloat16)
    raw_out = jnp.dot(out_w, hidden.T, preferred_element_type=jnp.float32) + out_b[:, None]
    raw_out = raw_out.reshape(4, ray_rows.shape[0], -1)
    position = jnp.arange(raw_out.shape[2], dtype=jnp.int32) // sample_rows.shape[0]
    occupied = (position[None, :] < occupied_count[:, None]).astype(jnp.float32)
    return inputs, preact, hidden, raw_out, occupied


def render(raw_out, occupied):
    optical = step_length * jax.nn.softplus(raw_out[0]) * occupied
    entered = jnp.cumsum(optical, axis=-1) - optical
    weight = jnp.exp(-entered) * (-jnp.expm1(-optical))
    shading = jax.nn.sigmoid(raw_out[1:])
    colors = jnp.sum(weight[None] * shading, axis=-1)
    through = jnp.exp(-jnp.sum(optical, axis=-1))
    return optical, entered, weight, shading, colors, through


def shade_backward(inputs, preact, hidden, raw_out, occupied, hidden_w, out_w, color_cot, trans_cot):
    optical, entered, weight, shading, colors, through = render(raw_out, occupied)
    q_term = jnp.sum(shading * color_cot[:, :, None], axis=0)
    q_weight = q_term * weight
    after_sum = jnp.sum(q_weight, axis=-1, keepdims=True) - jnp.cumsum(q_weight, axis=-1)
    grad_optical = q_term * jnp.exp(-(entered + optical)) - after_sum - (trans_cot * through)[:, None]
    grad_density = step_length * grad_optical * occupied * jax.nn.sigmoid(raw_out[0])
    grad_shade = weight[None] * color_cot[:, :, None] * shading * (1.0 - shading)
    grad_raw = jnp.concatenate([grad_density[None], grad_shade], axis=0).reshape(4, -1)
    raw_rounded = grad_raw.astype(jnp.bfloat16)
    grad_hidden = jnp.dot(raw_rounded.T, out_w, preferred_element_type=jnp.float32)
    grad_pre = jnp.where(preact > 0.0, grad_hidden, 0.0).astype(jnp.bfloat16)
    grad_w_out = jnp.dot(raw_rounded, hidden, preferred_element_type=jnp.float32)
    grad_b_out = jnp.sum(grad_raw, axis=1)
    grad_w_hidden = jnp.dot(inputs.T, grad_pre, preferred_element_type=jnp.float32)
    grad_b_hidden = jnp.sum(grad_pre.astype(jnp.float32), axis=0)
    grad_inputs = jnp.dot(grad_pre, hidden_w.T, preferred_element_type=jnp.float32)
    return grad_w_out, grad_b_out, grad_w_hidden, grad_b_hidden, grad_inputs


def combine_pair(first, second, order_flag):
    first_color, first_trans = first
    second_color, second_trans = second
    first_ahead = first_color + first_trans[None] * second_color
    second_ahead = second_color + second_trans[None] * first_color
    return jnp.where(order_flag[None], first_ahead, second_ahead), first_trans * second_trans


def composite(seg_color, seg_trans, direction):
    forward = direction == 0
    backward = direction == 1
    start = (jnp.zeros(seg_color.shape[1:], jnp.float32), jnp.ones(seg_trans.shape[1:], jnp.float32))

    def lower_step(totals, pieces):
        return combine_pair(totals, pieces, forward), totals

    def upper_step(totals, pieces):
        return combine_pair(totals, pieces, backward), totals

    ended, (low_color, low_trans) = lax.scan(lower_step, start, (seg_color, seg_trans))
    ended, (high_color, high_trans) = lax.scan(upper_step, start, (seg_color, seg_trans), reverse=True)
    return low_color, low_trans, high_color, high_trans


def reference(ray_code, direction, target, brick_code, sample_code, w_hidden, b_hidden, w_out, b_out, brick_ids, occupancy):
    total_rays = ray_code.shape[0]
    feature_width = ray_code.shape[1]
    block_rays = math.gcd(total_rays, 128)
    count_blocks = total_rays // block_rays
    ray_blocks = ray_code.reshape(count_blocks, block_rays, feature_width)
    slots = brick_ids.shape[1]

    def split_slab(slot_all, occ_all):
        id_blocks = slot_all.reshape(slots, count_blocks, block_rays).transpose(1, 0, 2)
        return id_blocks, occ_all.reshape(count_blocks, block_rays)

    def slab_forward(pieces):
        brick_rows, sample_rows, hidden_w, hidden_b, out_w, out_b, slot_all, occ_all = pieces
        id_blocks, occ_blocks = split_slab(slot_all, occ_all)

        def one_block(operands):
            ray_rows, slot_ids, occupied_count = operands
            inputs, preact, hidden, raw_out, occupied = shade_forward(
                brick_rows, sample_rows, ray_rows, slot_ids, occupied_count, hidden_w, hidden_b, out_w, out_b)
            rendered = render(raw_out, occupied)
            return rendered[4], rendered[5]

        colors_b, through_b = lax.map(one_block, (ray_blocks, id_blocks, occ_blocks))
        return colors_b.transpose(1, 0, 2).reshape(3, total_rays), through_b.reshape(total_rays)

    seg_color, seg_trans = lax.map(slab_forward, (brick_code, sample_code, w_hidden, b_hidden, w_out, b_out, brick_ids, occupancy))
    low_color, low_trans, high_color, high_trans = composite(seg_color, seg_trans, direction)
    forward = (direction == 0)[None, :]
    before_color = jnp.where(forward[:, None, :], low_color, high_color)
    before_trans = jnp.where(forward, low_trans, high_trans)
    after_color = jnp.where(forward[:, None, :], high_color, low_color)
    color = before_color[0] + before_trans[0][None, :] * (seg_color[0] + seg_trans[0][None, :] * after_color[0])
    residual_g = color - target
    cot_color = before_trans[:, None, :] * residual_g[None]
    cot_trans = before_trans * jnp.sum(after_color * residual_g[None], axis=1)

    def slab_backward(pieces):
        brick_rows, sample_rows, hidden_w, hidden_b, out_w, out_b, slot_all, occ_all, color_cot, trans_cot = pieces
        id_blocks, occ_blocks = split_slab(slot_all, occ_all)
        color_blocks = color_cot.reshape(3, count_blocks, block_rays).transpose(1, 0, 2)
        trans_blocks = trans_cot.reshape(count_blocks, block_rays)

        def one_block(totals, operands):
            ray_rows, slot_ids, occupied_count, block_color_cot, block_trans_cot = operands
            inputs, preact, hidden, raw_out, occupied = shade_forward(
                brick_rows, sample_rows, ray_rows, slot_ids, occupied_count, hidden_w, hidden_b, out_w, out_b)
            grad_w_out, grad_b_out, grad_w_hidden, grad_b_hidden, grad_inputs = shade_backward(
                inputs, preact, hidden, raw_out, occupied, hidden_w, out_w, block_color_cot, block_trans_cot)
            per_position = grad_inputs.reshape(block_rays, slots, sample_rows.shape[0], feature_width)
            per_slot = jnp.sum(per_position, axis=2)
            brick_sum = jax.ops.segment_sum(per_slot.reshape(-1, feature_width), slot_ids.T.reshape(-1),
                                            num_segments=brick_rows.shape[0])
            totals = (totals[0] + grad_w_out, totals[1] + grad_b_out, totals[2] + grad_w_hidden,
                      totals[3] + grad_b_hidden, totals[4] + jnp.sum(per_position, axis=(0, 1)), totals[5] + brick_sum)
            return totals, jnp.sum(per_slot, axis=1)

        start = (jnp.zeros((4, feature_width), jnp.float32), jnp.zeros((4,), jnp.float32),
                 jnp.zeros((feature_width, feature_width), jnp.float32), jnp.zeros((feature_width,), jnp.float32),
                 jnp.zeros((sample_rows.shape[0], feature_width), jnp.float32),
                 jnp.zeros((brick_rows.shape[0], feature_width), jnp.float32))
        totals, ray_grads = lax.scan(one_block, start, (ray_blocks, id_blocks, occ_blocks, color_blocks, trans_blocks))
        return totals + (ray_grads.reshape(total_rays, feature_width),)

    results = lax.map(slab_backward, (brick_code, sample_code, w_hidden, b_hidden, w_out, b_out, brick_ids, occupancy, cot_color, cot_trans))
    grad_w_out, grad_b_out, grad_w_hidden, grad_b_hidden, grad_sample, grad_brick, ray_all = results
    grad_ray = jnp.sum(ray_all, axis=0)
    return color, grad_ray, grad_brick, grad_sample, grad_w_hidden, grad_b_hidden, grad_w_out, grad_b_out
```

```python
import functools
import jax
import jax.numpy as jnp
from jax import lax
from jax.experimental import pallas as pl
from jax.experimental.pallas import tpu as pltpu
from jax.sharding import PartitionSpec as P

step_length = 0.002
f32 = jnp.float32
bf16 = jnp.bfloat16
MESH = pl.DeviceIdType.MESH


def mm(a, b):
    return lax.dot_general(a, b, (((1,), (0,)), ((), ())), preferred_element_type=f32)


def mt(a, b):
    return lax.dot_general(a, b, (((1,), (1,)), ((), ())), preferred_element_type=f32)


def split(x):
    hi = x.astype(bf16)
    return hi, (x - hi.astype(f32)).astype(bf16)


def mm_left(a, x):
    hi, lo = split(x)
    return mm(a, hi) + mm(a, lo)


def mt_right(x, b):
    hi, lo = split(x)
    return mt(hi, b) + mt(lo, b)


def triangle(n, strict_lower):
    row = lax.broadcasted_iota(jnp.int32, (n, n), 0)
    col = lax.broadcasted_iota(jnp.int32, (n, n), 1)
    keep = (row > col) if strict_lower else (row < col)
    return jnp.where(keep, 1.0, 0.0).astype(bf16)


def log1p_small(e):
    series = e * (1.0 - e * (0.5 - e * (1.0 / 3.0 - e * 0.25)))
    return jnp.where(e < 0.01, series, jnp.log(1.0 + e))


def one_minus_exp(o):
    series = o * (1.0 - o * (0.5 - o * (1.0 / 6.0 - o * (1.0 / 24.0))))
    return jnp.where(o < 0.03, series, 1.0 - jnp.exp(-o))


def sigmoid(x):
    return 1.0 / (1.0 + jnp.exp(-x))


def occupied_mask(occ, samples, positions):
    slot = lax.broadcasted_iota(jnp.int32, (positions, occ.shape[1]), 0) // samples
    return jnp.where(slot < occ, 1.0, 0.0)


def optical_of(raw0, occupied):
    soft = jnp.maximum(raw0, 0.0) + log1p_small(jnp.exp(-jnp.abs(raw0)))
    return step_length * soft * occupied


def forward_kernel(ray_ref, ids_ref, brick_ref, sample_ref, w_ref, bh_ref, wo_ref, bo_ref, occ_ref,
                   a_ref, nb_ref, raw_ref, seg_ref, abf_ref, corr_ref, left_ref):
    slots, rays = ids_ref.shape
    bricks, width = brick_ref.shape
    samples = sample_ref.shape[0]
    w = w_ref[...]
    w2 = jnp.concatenate([w, w], axis=0)
    lane = lax.broadcasted_iota(jnp.int32, (128, bricks), 1)
    for k in range(slots):
        for i in range(rays // 128):
            row = ids_ref[k : k + 1, i * 128 : (i + 1) * 128]
            col = jnp.broadcast_to(row, (128, 128)).T
            wide = jnp.concatenate([col] * (bricks // 128), axis=1)
            hot = jnp.where(wide == lane, 1.0, 0.0).astype(bf16)
            chosen = mm(hot, brick_ref[...]).astype(bf16)
            both = jnp.concatenate([chosen, ray_ref[i * 128 : (i + 1) * 128, :]], axis=1)
            a = mm(both, w2) + bh_ref[...]
            at = k * rays + i * 128
            a_ref[at : at + 128, :] = a
            abf_ref[at : at + 128, :] = a.astype(bf16)
    nb = -mm(sample_ref[...], w)
    nb_ref[...] = nb
    nbr = nb.astype(bf16).astype(f32)
    wo = wo_ref[...].astype(f32)
    row32 = lax.broadcasted_iota(jnp.int32, (32, width), 0) % 8
    wexp = jnp.concatenate([jnp.broadcast_to(wo[c : c + 1, :], (8, width)) for c in range(4)], axis=0)
    for q in range(8):
        left_ref[:, q * width : (q + 1) * width] = jnp.where(row32 == q, wexp, 0.0).astype(bf16)
    for c in range(4):
        corr_ref[c, :, :] = jnp.broadcast_to(
            bo_ref[0, c] - jnp.sum(nbr * wo[c : c + 1, :], axis=1, keepdims=True), (samples, 128)
        )

    def group(g, carry):
        k = g // (samples // 8)
        jg = g % (samples // 8)
        j0 = pl.multiple_of(jg * 8, 8)
        nb8 = nb_ref[pl.ds(j0, 8), :].astype(bf16)
        for rc in range(rays // 256):
            base = pl.multiple_of(k * rays + rc * 256, 256)
            ab = abf_ref[pl.ds(base, 256), :]
            acc = jnp.zeros((32, 256), f32)
            for q in range(0, 8, 2):
                h = jnp.concatenate(
                    [jnp.maximum(ab, nb8[q : q + 1, :]), jnp.maximum(ab, nb8[q + 1 : q + 2, :])], axis=1
                )
                acc = acc + mt(left_ref[:, q * width : (q + 2) * width], h)
            p0 = pl.multiple_of(g * 8, 8)
            for c in range(4):
                fix = corr_ref[c, pl.ds(j0, 8), :]
                fix = jnp.concatenate([fix, fix], axis=1)
                raw_ref[c, pl.ds(p0, 8), rc * 256 : (rc + 1) * 256] = acc[c * 8 : (c + 1) * 8, :] + fix
        return carry

    lax.fori_loop(0, slots * samples // 8, group, 0)

    positions = slots * samples
    below = triangle(positions, True)
    for rc in range(rays // 128):
        cols = slice(rc * 128, (rc + 1) * 128)
        occupied = occupied_mask(occ_ref[:, cols], samples, positions)
        optical = optical_of(raw_ref[0, :, cols], occupied)
        entered = mm_left(below, optical)
        weight = jnp.exp(-entered) * one_minus_exp(optical)
        for c in range(3):
            seg_ref[c : c + 1, cols] = jnp.sum(weight * sigmoid(raw_ref[c + 1, :, cols]), axis=0, keepdims=True)
        seg_ref[3:4, cols] = jnp.exp(-jnp.sum(optical, axis=0, keepdims=True))


def backward_kernel(allseg_ref, target_ref, dir_ref, raw_ref, a_ref, nb_ref, ids_ref, occ_ref, brick_ref, ray_ref,
                    sample_ref, w_ref, wo_ref,
                    color_ref, gray_ref, gbrick_ref, pay_ref,
                    gj_ref, gr_ref, s_ref, t_ref):
    slabs = allseg_ref.shape[0]
    slots, rays = ids_ref.shape
    bricks, width = brick_ref.shape
    samples = sample_ref.shape[0]
    positions = slots * samples
    own = rays // slabs
    me = lax.axis_index("slab")
    ahead = dir_ref[...] == 0
    zero3 = jnp.zeros((3, rays), f32)
    one1 = jnp.ones((1, rays), f32)

    def low_step(t, state):
        color, trans = state
        piece, through = allseg_ref[t, 0:3, :], allseg_ref[t, 3:4, :]
        color = jnp.where(ahead, color + trans * piece, piece + through * color)
        return color, trans * through

    def high_step(i, state):
        t = slabs - 1 - i
        color, trans = state
        piece, through = allseg_ref[t, 0:3, :], allseg_ref[t, 3:4, :]
        color = jnp.where(ahead, piece + through * color, color + trans * piece)
        return color, trans * through

    low_c, low_t = lax.fori_loop(0, me, low_step, (zero3, one1))
    high_c, high_t = lax.fori_loop(0, slabs - 1 - me, high_step, (zero3, one1))
    seg_c, seg_t = allseg_ref[me, 0:3, :], allseg_ref[me, 3:4, :]
    before_c = jnp.where(ahead, low_c, high_c)
    before_t = jnp.where(ahead, low_t, high_t)
    after_c = jnp.where(ahead, high_c, low_c)
    color = before_c + before_t * (seg_c + seg_t * after_c)
    residual = color - target_ref[...]
    cot_c = before_t * residual
    cot_t = before_t * jnp.sum(after_c * residual, axis=0, keepdims=True)
    tail = cot_t * seg_t
    color8 = jnp.concatenate([color, jnp.zeros((5, rays), f32)], axis=0)
    color_ref[...] = pltpu.roll(color8, lax.rem(rays - me * own, rays), 1)[0:3, 0:own]

    below = triangle(positions, True)
    above = triangle(positions, False)
    lane_row = lax.broadcasted_iota(jnp.int32, (1, width), 1)
    bout = jnp.zeros((1, width), f32)
    for rc in range(rays // 128):
        cols = slice(rc * 128, (rc + 1) * 128)
        occupied = occupied_mask(occ_ref[:, cols], samples, positions)
        raw0 = raw_ref[0, :, cols]
        optical = optical_of(raw0, occupied)
        entered = mm_left(below, optical)
        weight = jnp.exp(-entered) * one_minus_exp(optical)
        q_term = jnp.zeros((positions, 128), f32)
        grads = []
        for c in range(3):
            shade = sigmoid(raw_ref[c + 1, :, cols])
            lit = shade * cot_c[c : c + 1, cols]
            q_term = q_term + lit
            grads.append(weight * lit * (1.0 - shade))
        after = mm_left(above, q_term * weight)
        grad_optical = q_term * jnp.exp(-(entered + optical)) - after - tail[:, cols]
        grads = [step_length * grad_optical * occupied * sigmoid(raw0)] + grads
        for c in range(4):
            g = grads[c]
            bout = bout + jnp.where(lane_row == c, jnp.sum(g), 0.0)
            for k in range(slots):
                block = k * (rays // 128) + rc
                gj_ref[block, pl.ds(c, samples, stride=4), :] = g[k * samples : (k + 1) * samples, :]
            gr_ref[pl.ds(rc * 512 + c, 128, stride=4), :] = g.T

    def sample_pair(jp, carry):
        row8 = pl.multiple_of(jp * 8, 8)
        n0 = nb_ref[pl.ds(jp * 2, 1), :]
        n1 = nb_ref[pl.ds(jp * 2 + 1, 1), :]
        acc = jnp.zeros((8, 2 * width), f32)
        for i in range(slots * rays // 256):
            a = a_ref[i * 256 : (i + 1) * 256, :]
            m = jnp.concatenate(
                [jnp.where(a > n0, 1.0, 0.0).astype(bf16), jnp.where(a > n1, 1.0, 0.0).astype(bf16)], axis=1
            )
            left = jnp.concatenate([gj_ref[2 * i, pl.ds(row8, 8), :], gj_ref[2 * i + 1, pl.ds(row8, 8), :]], axis=1)
            acc = acc + mm(left.astype(bf16), m)
        sub = lax.broadcasted_iota(jnp.int32, (8, width), 0)
        t_ref[pl.ds(row8, 8), :] = jnp.where(sub < 4, acc[:, :width], acc[:, width:])
        return carry

    lax.fori_loop(0, samples // 2, sample_pair, 0)

    nb = nb_ref[...]
    lane_p = lax.broadcasted_iota(jnp.int32, (8, positions), 1)
    sub8 = lax.broadcasted_iota(jnp.int32, (8, width), 0)

    def ray_group(rg, carry):
        r0 = pl.multiple_of(rg * 8, 8)
        a0 = a_ref[pl.ds(r0, 8), :]
        a1 = a_ref[pl.ds(rays + r0, 8), :]
        for i in range(0, 8, 2):
            halves = []
            for r in (i, i + 1):
                m0 = jnp.where(a0[r : r + 1, :] > nb, 1.0, 0.0).astype(bf16)
                m1 = jnp.where(a1[r : r + 1, :] > nb, 1.0, 0.0).astype(bf16)
                halves.append(jnp.concatenate([m0, m1], axis=0))
            m = jnp.concatenate(halves, axis=1)
            at = pl.multiple_of(r0 * 4 + i * 4, 8)
            g8 = gr_ref[pl.ds(at, 8), :]
            left = jnp.concatenate(
                [jnp.where(lane_p < samples, g8, 0.0), jnp.where(lane_p < samples, 0.0, g8)], axis=0
            ).astype(bf16)
            out = mm(left, m)
            for k in range(2):
                part = out[k * 8 : (k + 1) * 8, :]
                s_ref[k, pl.ds(at, 8), :] = jnp.where(sub8 < 4, part[:, :width], part[:, width:])
        return carry

    lax.fori_loop(0, rays // 8, ray_group, 0)

    wo = wo_ref[...].astype(f32)
    w = w_ref[...]
    gw_out = []
    ga = [jnp.zeros((rays, width), f32) for _ in range(slots)]
    gb = jnp.zeros((samples, width), f32)
    for c in range(4):
        t_c = t_ref[pl.ds(c, samples, stride=4), :]
        gb = gb + t_c * wo[c : c + 1, :]
        total = -jnp.sum(t_c * nb, axis=0, keepdims=True)
        for k in range(slots):
            s_c = s_ref[k, pl.ds(c, rays, stride=4), :]
            ga[k] = ga[k] + s_c * wo[c : c + 1, :]
            total = total + jnp.sum(s_c * a_ref[k * rays : (k + 1) * rays, :], axis=0, keepdims=True)
        gw_out.append(total)
    ga_sum = ga[0] + ga[1]
    gray_ref[...] = mt_right(ga_sum, w).astype(gray_ref.dtype)
    ga_parts = [jnp.concatenate(split(ga[k]), axis=1) for k in range(slots)]
    ga_all = jnp.concatenate(ga_parts, axis=0)
    gbp = []
    for bt in range(bricks // 128):
        sub = lax.broadcasted_iota(jnp.int32, (128, rays), 0) + bt * 128
        hot = jnp.concatenate(
            [jnp.where(ids_ref[k : k + 1, :] == sub, 1.0, 0.0).astype(bf16) for k in range(slots)], axis=1
        )
        pre = mm(hot, ga_all)
        pre = pre[:, :width] + pre[:, width:]
        gbp.append(pre)
        gbrick_ref[bt * 128 : (bt + 1) * 128, :] = mt_right(pre, w).astype(gbrick_ref.dtype)
    right = jnp.concatenate(gbp + [ga_sum, gb], axis=0)
    right = jnp.concatenate(split(right), axis=1)
    left = jnp.concatenate([brick_ref[...], ray_ref[...], sample_ref[...]], axis=0).astype(f32).T.astype(bf16)
    gw = mm(left, right)
    pay_ref[0:samples, :] = mt_right(gb, w)
    pay_ref[samples : samples + width, :] = gw[:, :width] + gw[:, width:]
    rest = gw_out + [jnp.sum(gb, axis=0, keepdims=True), bout]
    base = samples + width
    pay_ref[base : base + 8, :] = jnp.concatenate(rest + [jnp.zeros((2, width), f32)], axis=0)
    pay_ref[base + 8 :, :] = jnp.zeros((pay_ref.shape[0] - base - 8, width), f32)


def greet(axes):
    barrier = pltpu.get_barrier_semaphore()
    total = 0
    for name, n in axes:
        me = lax.axis_index(name)

        def hello(i, carry, name=name, n=n, me=me):
            pl.semaphore_signal(barrier, inc=1, device_id={name: lax.rem(me + i, n)}, device_id_type=MESH)
            return carry

        lax.fori_loop(1, n, hello, 0)
        total += n - 1
    pl.semaphore_wait(barrier, total)


def spread(name, n, src_of, dst_of, send, recv):
    me = lax.axis_index(name)

    def copy_to(peer, slot):
        return pltpu.make_async_remote_copy(
            src_ref=src_of(peer), dst_ref=dst_of(slot), send_sem=send.at[peer], recv_sem=recv.at[slot],
            device_id={name: peer}, device_id_type=MESH,
        )

    def start(i, carry):
        copy_to(lax.rem(me + i, n), me).start()
        return carry

    def wait_recv(i, carry):
        peer = lax.rem(me + i, n)
        copy_to(peer, peer).wait_recv()
        return carry

    def wait_send(i, carry):
        peer = lax.rem(me + i, n)
        copy_to(peer, me).wait_send()
        return carry

    return (
        lambda: lax.fori_loop(1, n, start, 0),
        lambda: lax.fori_loop(1, n, wait_recv, 0),
        lambda: lax.fori_loop(1, n, wait_send, 0),
    )


def gather_kernel(n, x_ref, out_ref, send, recv, local):
    me = lax.axis_index("slab")
    mine = pltpu.make_async_copy(x_ref, out_ref.at[me], local)
    mine.start()
    greet([("slab", n)])
    start, wait_recv, wait_send = spread(
        "slab", n, lambda peer: x_ref, lambda slot: out_ref.at[slot], send, recv
    )
    start()
    wait_recv()
    wait_send()
    mine.wait()


def gather_slab(x, n, cid):
    return pl.pallas_call(
        functools.partial(gather_kernel, n),
        out_shape=jax.ShapeDtypeStruct((n,) + x.shape, x.dtype),
        in_specs=[pl.BlockSpec(memory_space=pltpu.VMEM)],
        out_specs=pl.BlockSpec(memory_space=pltpu.VMEM),
        scratch_shapes=[
            pltpu.SemaphoreType.DMA((n,)),
            pltpu.SemaphoreType.DMA((n,)),
            pltpu.SemaphoreType.DMA,
        ],
        compiler_params=pltpu.CompilerParams(collective_id=cid, has_side_effects=True),
    )(x)


def reduce_kernel(ns, nr, gray_ref, gbrick_ref, pay_ref,
                  oray_ref, obrick_ref, osample_ref, owh_ref, obh_ref, owo_ref, obo_ref,
                  rbuf, bbuf, pbuf, psum, pall,
                  rs_send, rs_recv, bs_send, bs_recv, ps_send, ps_recv, ag_send, ag_recv):
    me_s = lax.axis_index("slab")
    me_r = lax.axis_index("ray")
    own = rbuf.shape[1]
    share = bbuf.shape[1]
    part = pbuf.shape[1]
    greet([("slab", ns), ("ray", nr)])

    def rows(ref, index, size):
        return ref.at[pl.ds(pl.multiple_of(index * size, 8), size), :]

    p_start, p_recv, p_sent = spread(
        "ray", nr, lambda peer: rows(pay_ref, peer, part), lambda slot: pbuf.at[slot], ps_send, ps_recv
    )
    r_start, r_recv, r_sent = spread(
        "slab", ns, lambda peer: rows(gray_ref, peer, own), lambda slot: rbuf.at[slot], rs_send, rs_recv
    )
    b_start, b_recv, b_sent = spread(
        "ray", nr, lambda peer: rows(gbrick_ref, peer, share), lambda slot: bbuf.at[slot], bs_send, bs_recv
    )
    a_start, a_recv, a_sent = spread(
        "ray", nr, lambda peer: psum, lambda slot: pall.at[slot], ag_send, ag_recv
    )
    p_start()
    r_start()
    b_start()
    pbuf[me_r, :, :] = pay_ref[pl.ds(pl.multiple_of(me_r * part, 8), part), :]
    rbuf[me_s, :, :] = gray_ref[pl.ds(pl.multiple_of(me_s * own, 8), own), :]
    bbuf[me_r, :, :] = gbrick_ref[pl.ds(pl.multiple_of(me_r * share, 8), share), :]
    p_recv()
    total = pbuf[0, :, :]
    for i in range(1, nr):
        total = total + pbuf[i, :, :]
    psum[...] = total
    pall[me_r, :, :] = total
    a_start()
    r_recv()
    total = rbuf[0, :, :].astype(f32)
    for i in range(1, ns):
        total = total + rbuf[i, :, :].astype(f32)
    oray_ref[...] = total
    b_recv()
    total = bbuf[0, :, :].astype(f32)
    for i in range(1, nr):
        total = total + bbuf[i, :, :].astype(f32)
    obrick_ref[0, :, :] = total
    a_recv()

    def piece(lo, hi):
        out = []
        while lo < hi:
            slot, off = lo // part, lo % part
            size = min(part - off, hi - lo)
            out.append(pall[slot, off : off + size, :])
            lo += size
        return out[0] if len(out) == 1 else jnp.concatenate(out, axis=0)

    samples, width = osample_ref.shape[1], osample_ref.shape[2]
    base = samples + width
    osample_ref[0, :, :] = piece(0, samples)
    owh_ref[0, :, :] = piece(samples, base)
    rest = piece(base, base + 8)
    owo_ref[0, :, :] = rest[0:4, :]
    obh_ref[...] = rest[4:5, :]
    obo_ref[...] = rest[5:6, 0:4]
    p_sent()
    r_sent()
    b_sent()
    a_sent()


def body(ray_code, direction, target, brick_code, sample_code, w_hidden, b_hidden, w_out, b_out, brick_ids, occupancy):
    ns = lax.axis_size("slab")
    nr = lax.axis_size("ray")
    width = ray_code.shape[1]
    rays = direction.shape[0]
    slots = brick_ids.shape[1]
    bricks = brick_code.shape[1]
    samples = sample_code.shape[1]
    positions = slots * samples
    own = rays // ns
    share = bricks // nr
    vm = pl.BlockSpec(memory_space=pltpu.VMEM)
    sm = pl.BlockSpec(memory_space=pltpu.SMEM)
    params = pltpu.CompilerParams(vmem_limit_bytes=56 * 1024 * 1024)

    ray_rows = gather_slab(ray_code, ns, 0).reshape(rays, width)
    brick, sample, w, wo, ids = brick_code[0], sample_code[0], w_hidden[0], w_out[0], brick_ids[0]
    a, nb, raw, seg = pl.pallas_call(
        forward_kernel,
        out_shape=(
            jax.ShapeDtypeStruct((slots * rays, width), f32),
            jax.ShapeDtypeStruct((samples, width), f32),
            jax.ShapeDtypeStruct((4, positions, rays), f32),
            jax.ShapeDtypeStruct((4, rays), f32),
        ),
        in_specs=[vm, vm, vm, vm, vm, vm, vm, sm, vm],
        out_specs=(vm, vm, vm, vm),
        scratch_shapes=[
            pltpu.VMEM((slots * rays, width), bf16),
            pltpu.VMEM((4, samples, 128), f32),
            pltpu.VMEM((32, 8 * width), bf16),
        ],
        compiler_params=params,
    )(ray_rows, ids, brick, sample, w, b_hidden, wo, b_out, occupancy)
    allseg = gather_slab(seg, ns, 1)
    color, gray, gbrick, pay = pl.pallas_call(
        backward_kernel,
        out_shape=(
            jax.ShapeDtypeStruct((3, own), f32),
            jax.ShapeDtypeStruct((rays, width), f32),
            jax.ShapeDtypeStruct((bricks, width), f32),
            jax.ShapeDtypeStruct((256, width), f32),
        ),
        in_specs=[vm] * 13,
        out_specs=(vm, vm, vm, vm),
        scratch_shapes=[
            pltpu.VMEM((slots * rays // 128, 4 * samples, 128), f32),
            pltpu.VMEM((4 * rays, positions), f32),
            pltpu.VMEM((slots, 4 * rays, width), f32),
            pltpu.VMEM((4 * samples, width), f32),
        ],
        compiler_params=params,
    )(allseg, target, direction[None, :], raw, a, nb, ids, occupancy, brick, ray_rows, sample, w, wo)
    part = pay.shape[0] // nr
    sem = lambda n: pltpu.SemaphoreType.DMA((n,))
    outs = pl.pallas_call(
        functools.partial(reduce_kernel, ns, nr),
        out_shape=(
            jax.ShapeDtypeStruct((own, width), f32),
            jax.ShapeDtypeStruct((1, share, width), f32),
            jax.ShapeDtypeStruct((1, samples, width), f32),
            jax.ShapeDtypeStruct((1, width, width), f32),
            jax.ShapeDtypeStruct((1, width), f32),
            jax.ShapeDtypeStruct((1, 4, width), f32),
            jax.ShapeDtypeStruct((1, 4), f32),
        ),
        in_specs=[vm] * 3,
        out_specs=(vm,) * 7,
        scratch_shapes=[
            pltpu.VMEM((ns, own, width), gray.dtype),
            pltpu.VMEM((nr, share, width), gbrick.dtype),
            pltpu.VMEM((nr, part, width), f32),
            pltpu.VMEM((part, width), f32),
            pltpu.VMEM((nr, part, width), f32),
            sem(ns), sem(ns), sem(nr), sem(nr), sem(nr), sem(nr), sem(nr), sem(nr),
        ],
        compiler_params=pltpu.CompilerParams(collective_id=2, has_side_effects=True),
    )(gray, gbrick, pay)
    return (color,) + tuple(outs)


def solution(mesh):
    in_specs = (
        P(("ray", "slab"), None),
        P("ray"),
        P(None, "ray"),
        P("slab", None, None),
        P("slab", None, None),
        P("slab", None, None),
        P("slab", None),
        P("slab", None, None),
        P("slab", None),
        P("slab", None, "ray"),
        P("slab", "ray"),
    )
    out_specs = (
        P(None, ("ray", "slab")),
        P(("ray", "slab"), None),
        P("slab", "ray", None),
        P("slab", None, None),
        P("slab", None, None),
        P("slab", None),
        P("slab", None, None),
        P("slab", None),
    )
    return jax.shard_map(body, mesh=mesh, in_specs=in_specs, out_specs=out_specs, check_vma=False)
```

```python
import functools
import jax
import jax.numpy as jnp
from jax import lax
from jax.experimental import pallas as pl
from jax.experimental.pallas import tpu as pltpu
from jax.sharding import PartitionSpec as P

step_length = 0.002
f32 = jnp.float32
bf16 = jnp.bfloat16
MESH = pl.DeviceIdType.MESH


def mm(a, b):
    return lax.dot_general(a, b, (((1,), (0,)), ((), ())), preferred_element_type=f32)


def mt(a, b):
    return lax.dot_general(a, b, (((1,), (1,)), ((), ())), preferred_element_type=f32)


def split(x):
    hi = x.astype(bf16)
    return hi, (x - hi.astype(f32)).astype(bf16)


def mm_left(a, x):
    hi, lo = split(x)
    return mm(a, hi) + mm(a, lo)


def mt_right(x, b):
    hi, lo = split(x)
    return mt(hi, b) + mt(lo, b)


def triangle(n, strict_lower):
    row = lax.broadcasted_iota(jnp.int32, (n, n), 0)
    col = lax.broadcasted_iota(jnp.int32, (n, n), 1)
    keep = (row > col) if strict_lower else (row < col)
    return jnp.where(keep, 1.0, 0.0).astype(bf16)


def log1p_small(e):
    series = e * (1.0 - e * (0.5 - e * (1.0 / 3.0 - e * 0.25)))
    return jnp.where(e < 0.01, series, jnp.log(1.0 + e))


def one_minus_exp(o):
    series = o * (1.0 - o * (0.5 - o * (1.0 / 6.0 - o * (1.0 / 24.0))))
    return jnp.where(o < 0.03, series, 1.0 - jnp.exp(-o))


def sigmoid(x):
    return 0.5 * jnp.tanh(0.5 * x) + 0.5


def occupied_mask(occ, samples, positions):
    slot = lax.broadcasted_iota(jnp.int32, (positions, occ.shape[1]), 0) // samples
    return jnp.where(slot < occ, 1.0, 0.0)


def optical_of(raw0, occupied):
    soft = jnp.maximum(raw0, 0.0) + log1p_small(jnp.exp(-jnp.abs(raw0)))
    return step_length * soft * occupied


def signal_peers(axes):
    barrier = pltpu.get_barrier_semaphore()
    for name, n in axes:
        me = lax.axis_index(name)

        def hello(i, carry, name=name, n=n, me=me):
            pl.semaphore_signal(barrier, inc=1, device_id={name: lax.rem(me + i, n)}, device_id_type=MESH)
            return carry

        lax.fori_loop(1, n, hello, 0)


def await_peers(axes):
    pl.semaphore_wait(pltpu.get_barrier_semaphore(), sum(n - 1 for _, n in axes))


class Exchange:
    def __init__(self, name, n, src_of, dst_of, send, recv):
        self.name, self.n, self.src_of, self.dst_of, self.send, self.recv = name, n, src_of, dst_of, send, recv
        self.me = lax.axis_index(name)

    def copy(self, peer, slot):
        return pltpu.make_async_remote_copy(
            src_ref=self.src_of(peer), dst_ref=self.dst_of(slot), send_sem=self.send.at[peer],
            recv_sem=self.recv.at[slot], device_id={self.name: peer}, device_id_type=MESH,
        )

    def each(self, act, first=0, count=None):
        count = self.n if count is None else count

        def step(i, carry):
            peer = first + lax.rem(self.me + i, count)

            @pl.when(peer != self.me)
            def _():
                act(peer)

            return carry

        lax.fori_loop(0, count, step, 0)

    def start(self, first=0, count=None):
        self.each(lambda peer: self.copy(peer, self.me).start(), first, count)

    def wait_recv(self):
        self.each(lambda peer: self.copy(peer, peer).wait_recv())

    def wait_send(self, first=0, count=None):
        self.each(lambda peer: self.copy(peer, self.me).wait_send(), first, count)


def step_kernel(ns, nr, x_ref, dir_ref, target_ref, brick_ref, sample_ref, w_ref, bh_ref, wo_ref, bo_ref, ids_ref,
                occ_ref,
                color_ref, oray_ref, obrick_ref, opay_ref,
                ray_ref, xg_ref, a_ref, abf_ref, nb_ref, corr_ref, left_ref, raw_ref, weight_ref, trail_ref,
                seg_ref, allseg_ref, gj_ref, gr_ref, s_ref, t_ref, ga_ref, gray_ref, gbrick_ref, pay_ref,
                rbuf, bbuf, pbuf, psum,
                xs_send, xs_recv, ss_send, ss_recv, rs_send, rs_recv, bs_send, bs_recv, ps_send, ps_recv,
                ag_send, ag_recv):
    slots, rays = ids_ref.shape
    bricks, width = brick_ref.shape
    samples = sample_ref.shape[0]
    positions = slots * samples
    own = rays // ns
    share = bricks // nr
    part = psum.shape[0]
    half = rays // 2
    me = lax.axis_index("slab")
    me_r = lax.axis_index("ray")
    axes = [("slab", ns), ("ray", nr)]

    def rows(ref, index, size):
        return ref.at[pl.ds(pl.multiple_of(index * size, 8), size), :]

    x_ex = Exchange("slab", ns, lambda peer: x_ref, lambda slot: rows(ray_ref, slot, own), xs_send, xs_recv)
    s_ex = [
        Exchange(
            "slab", ns, lambda peer, h=h: seg_ref.at[h], lambda slot, h=h: allseg_ref.at[h, slot],
            ss_send.at[h], ss_recv.at[h],
        )
        for h in range(2)
    ]
    r_ex = Exchange("slab", ns, lambda peer: rows(gray_ref, peer, own), lambda slot: rbuf.at[slot], rs_send, rs_recv)
    b_ex = Exchange("ray", nr, lambda peer: rows(gbrick_ref, peer, share), lambda slot: bbuf.at[slot], bs_send, bs_recv)
    p_ex = Exchange("ray", nr, lambda peer: rows(pay_ref, peer, part), lambda slot: pbuf.at[slot], ps_send, ps_recv)
    a_ex = Exchange("ray", nr, lambda peer: psum, lambda slot: rows(opay_ref, slot, part), ag_send, ag_recv)

    signal_peers(axes)
    w = w_ref[...]
    w2 = jnp.concatenate([w, w], axis=0)
    nb = -mm(sample_ref[...], w)
    nb_ref[...] = nb
    nbr = nb.astype(bf16).astype(f32)
    wo = wo_ref[...].astype(f32)
    row32 = lax.broadcasted_iota(jnp.int32, (32, width), 0) % 8
    wexp = jnp.concatenate([jnp.broadcast_to(wo[c : c + 1, :], (8, width)) for c in range(4)], axis=0)
    for q in range(8):
        left_ref[:, q * width : (q + 1) * width] = jnp.where(row32 == q, wexp, 0.0).astype(bf16)
    for c in range(4):
        corr_ref[c, :, :] = jnp.broadcast_to(
            bo_ref[0, c] - jnp.sum(nbr * wo[c : c + 1, :], axis=1, keepdims=True), (samples, 128)
        )
    await_peers(axes)
    x_ex.start()
    ray_ref[pl.ds(pl.multiple_of(me * own, 8), own), :] = x_ref[...]
    lane = lax.broadcasted_iota(jnp.int32, (128, bricks), 1)
    for k in range(slots):
        for i in range(rays // 128):
            row = ids_ref[k : k + 1, i * 128 : (i + 1) * 128]
            col = jnp.broadcast_to(row, (128, 128)).T
            wide = jnp.concatenate([col] * (bricks // 128), axis=1)
            hot = jnp.where(wide == lane, 1.0, 0.0).astype(bf16)
            at = k * rays + i * 128
            xg_ref[at : at + 128, :] = mm(hot, brick_ref[...]).astype(bf16)
    x_ex.wait_recv()

    below = triangle(positions, True)
    above = triangle(positions, False)

    def shade_half(h):
        for k in range(slots):
            at = k * rays + h * half
            both = jnp.concatenate([xg_ref[at : at + half, :], ray_ref[h * half : (h + 1) * half, :]], axis=1)
            a = mm(both, w2) + bh_ref[...]
            a_ref[at : at + half, :] = a
            abf_ref[at : at + half, :] = a.astype(bf16)

        def group(g, carry):
            k = g // (samples // 8)
            j0 = pl.multiple_of((g % (samples // 8)) * 8, 8)
            nb8 = nb_ref[pl.ds(j0, 8), :].astype(bf16)
            base = pl.multiple_of(k * rays + h * half, half)
            ab = abf_ref[pl.ds(base, half), :]
            acc = jnp.zeros((32, half), f32)
            for q in range(0, 8, 2):
                hid = jnp.concatenate(
                    [jnp.maximum(ab, nb8[q : q + 1, :]), jnp.maximum(ab, nb8[q + 1 : q + 2, :])], axis=1
                )
                acc = acc + mt(left_ref[:, q * width : (q + 2) * width], hid)
            p0 = pl.multiple_of(g * 8, 8)
            for c in range(4):
                fix = corr_ref[c, pl.ds(j0, 8), :]
                fix = jnp.concatenate([fix] * (half // 128), axis=1)
                raw_ref[c, pl.ds(p0, 8), h * half : (h + 1) * half] = acc[c * 8 : (c + 1) * 8, :] + fix
            return carry

        lax.fori_loop(0, slots * samples // 8, group, 0)

        for rc in range(h * half // 128, (h + 1) * half // 128):
            cols = slice(rc * 128, (rc + 1) * 128)
            at = slice(rc * 128 - h * half, (rc + 1) * 128 - h * half)
            raw0 = raw_ref[0, :, cols]
            occupied = occupied_mask(occ_ref[:, cols], samples, positions)
            optical = optical_of(raw0, occupied)
            entered = mm_left(below, optical)
            weight = jnp.exp(-entered) * one_minus_exp(optical)
            weight_ref[:, cols] = weight
            trail_ref[:, cols] = jnp.exp(-(entered + optical))
            raw_ref[0, :, cols] = step_length * occupied * sigmoid(raw0)
            seg = []
            for c in range(3):
                shade = sigmoid(raw_ref[c + 1, :, cols])
                raw_ref[c + 1, :, cols] = shade
                seg.append(jnp.sum(weight * shade, axis=0, keepdims=True))
            seg.append(jnp.exp(-jnp.sum(optical, axis=0, keepdims=True)))
            seg = jnp.concatenate(seg, axis=0)
            seg_ref[h, :, at] = seg
            allseg_ref[h, me, :, at] = seg

    zero3 = jnp.zeros((3, half), f32)
    one1 = jnp.ones((1, half), f32)
    lane_row = lax.broadcasted_iota(jnp.int32, (1, width), 1)

    def render_half(h, bout):
        ahead = dir_ref[:, h * half : (h + 1) * half] == 0

        def low_step(t, state):
            color, trans = state
            piece, through = allseg_ref[h, t, 0:3, :], allseg_ref[h, t, 3:4, :]
            color = jnp.where(ahead, color + trans * piece, piece + through * color)
            return color, trans * through

        def high_step(i, state):
            t = ns - 1 - i
            color, trans = state
            piece, through = allseg_ref[h, t, 0:3, :], allseg_ref[h, t, 3:4, :]
            color = jnp.where(ahead, piece + through * color, color + trans * piece)
            return color, trans * through

        low_c, low_t = lax.fori_loop(0, me, low_step, (zero3, one1))
        high_c, high_t = lax.fori_loop(0, ns - 1 - me, high_step, (zero3, one1))
        seg_c, seg_t = allseg_ref[h, me, 0:3, :], allseg_ref[h, me, 3:4, :]
        before_c = jnp.where(ahead, low_c, high_c)
        before_t = jnp.where(ahead, low_t, high_t)
        after_c = jnp.where(ahead, high_c, low_c)
        color = before_c + before_t * (seg_c + seg_t * after_c)
        residual = color - target_ref[:, h * half : (h + 1) * half]
        cot_c = before_t * residual
        tail = before_t * jnp.sum(after_c * residual, axis=0, keepdims=True) * seg_t
        for i in range(half // 128):
            rc = h * (half // 128) + i
            cols = slice(rc * 128, (rc + 1) * 128)
            here = slice(i * 128, (i + 1) * 128)
            weight = weight_ref[:, cols]
            q_term = jnp.zeros((positions, 128), f32)
            grads = []
            for c in range(3):
                shade = raw_ref[c + 1, :, cols]
                lit = shade * cot_c[c : c + 1, here]
                q_term = q_term + lit
                grads.append(weight * lit * (1.0 - shade))
            after = mm_left(above, q_term * weight)
            grad_optical = q_term * trail_ref[:, cols] - after - tail[:, here]
            grads = [grad_optical * raw_ref[0, :, cols]] + grads
            for c in range(4):
                g = grads[c]
                bout = bout + jnp.where(lane_row == c, jnp.sum(g), 0.0)
                for k in range(slots):
                    block = k * (rays // 128) + rc
                    gj_ref[block, pl.ds(c, samples, stride=4), :] = g[k * samples : (k + 1) * samples, :]
                gr_ref[pl.ds(rc * 512 + c, 128, stride=4), :] = g.T
        return color, bout

    lane_p = lax.broadcasted_iota(jnp.int32, (8, positions), 1)
    sub8 = lax.broadcasted_iota(jnp.int32, (8, width), 0)

    def ray_group(rg, carry):
        r0 = pl.multiple_of(rg * 8, 8)
        a0 = a_ref[pl.ds(r0, 8), :]
        a1 = a_ref[pl.ds(rays + r0, 8), :]
        for i in range(0, 8, 2):
            halves = []
            for r in (i, i + 1):
                m0 = jnp.where(a0[r : r + 1, :] > nb, 1.0, 0.0).astype(bf16)
                m1 = jnp.where(a1[r : r + 1, :] > nb, 1.0, 0.0).astype(bf16)
                halves.append(jnp.concatenate([m0, m1], axis=0))
            m = jnp.concatenate(halves, axis=1)
            at = pl.multiple_of(r0 * 4 + i * 4, 8)
            g8 = gr_ref[pl.ds(at, 8), :]
            left = jnp.concatenate(
                [jnp.where(lane_p < samples, g8, 0.0), jnp.where(lane_p < samples, 0.0, g8)], axis=0
            ).astype(bf16)
            out = mm(left, m)
            for k in range(2):
                one = out[k * 8 : (k + 1) * 8, :]
                s_ref[k, pl.ds(at, 8), :] = jnp.where(sub8 < 4, one[:, :width], one[:, width:])
        return carry

    def rays_half(h, gw_out):
        lax.fori_loop(h * half // 8, (h + 1) * half // 8, ray_group, 0)
        ga = [jnp.zeros((half, width), f32) for _ in range(slots)]
        gw_out = list(gw_out)
        for c in range(4):
            for k in range(slots):
                s_c = s_ref[k, pl.ds(h * half * 4 + c, half, stride=4), :]
                ga[k] = ga[k] + s_c * wo[c : c + 1, :]
                at = k * rays + h * half
                gw_out[c] = gw_out[c] + jnp.sum(s_c * a_ref[at : at + half, :], axis=0, keepdims=True)
        for k in range(slots):
            at = k * rays + h * half
            ga_ref[at : at + half, :] = ga[k]
        gray_ref[h * half : (h + 1) * half, :] = mt_right(ga[0] + ga[1], w).astype(gray_ref.dtype)
        return gw_out

    def sample_pair(jp, carry):
        row8 = pl.multiple_of(jp * 8, 8)
        n0 = nb_ref[pl.ds(jp * 2, 1), :]
        n1 = nb_ref[pl.ds(jp * 2 + 1, 1), :]
        acc = jnp.zeros((8, 2 * width), f32)
        for i in range(slots * rays // 256):
            a = a_ref[i * 256 : (i + 1) * 256, :]
            m = jnp.concatenate(
                [jnp.where(a > n0, 1.0, 0.0).astype(bf16), jnp.where(a > n1, 1.0, 0.0).astype(bf16)], axis=1
            )
            left = jnp.concatenate([gj_ref[2 * i, pl.ds(row8, 8), :], gj_ref[2 * i + 1, pl.ds(row8, 8), :]], axis=1)
            acc = acc + mm(left.astype(bf16), m)
        t_ref[pl.ds(row8, 8), :] = jnp.where(sub8 < 4, acc[:, :width], acc[:, width:])
        return carry

    shade_half(0)
    s_ex[0].start()
    shade_half(1)
    s_ex[1].start()
    bout = jnp.zeros((1, width), f32)
    gw_out = [jnp.zeros((1, width), f32) for _ in range(4)]
    colors = []
    for h in range(2):
        s_ex[h].wait_recv()
        color, bout = render_half(h, bout)
        colors.append(color)
        gw_out = rays_half(h, gw_out)
        r_ex.start(h * (ns // 2), ns // 2)
    color8 = jnp.concatenate(
        [jnp.concatenate(colors, axis=1), jnp.zeros((5, rays), f32)], axis=0
    )
    color_ref[...] = pltpu.roll(color8, lax.rem(rays - me * own, rays), 1)[0:3, 0:own]
    rbuf[me, :, :] = gray_ref[pl.ds(pl.multiple_of(me * own, 8), own), :]

    ga_all = jnp.concatenate(split(ga_ref[...]), axis=1)
    gbp = []
    for bt in range(bricks // 128):
        sub = lax.broadcasted_iota(jnp.int32, (128, rays), 0) + bt * 128
        hot = jnp.concatenate(
            [jnp.where(ids_ref[k : k + 1, :] == sub, 1.0, 0.0).astype(bf16) for k in range(slots)], axis=1
        )
        pre = mm(hot, ga_all)
        pre = pre[:, :width] + pre[:, width:]
        gbp.append(pre)
        gbrick_ref[bt * 128 : (bt + 1) * 128, :] = mt_right(pre, w).astype(gbrick_ref.dtype)
    b_ex.start()
    bbuf[me_r, :, :] = gbrick_ref[pl.ds(pl.multiple_of(me_r * share, 8), share), :]

    lax.fori_loop(0, samples // 2, sample_pair, 0)
    gb = jnp.zeros((samples, width), f32)
    for c in range(4):
        t_c = t_ref[pl.ds(c, samples, stride=4), :]
        gb = gb + t_c * wo[c : c + 1, :]
        gw_out[c] = gw_out[c] - jnp.sum(t_c * nb, axis=0, keepdims=True)
    right = jnp.concatenate(gbp + [ga_ref[0:rays, :] + ga_ref[rays:, :], gb], axis=0)
    right = jnp.concatenate(split(right), axis=1)
    left = jnp.concatenate([brick_ref[...], ray_ref[...], sample_ref[...]], axis=0).astype(f32).T.astype(bf16)
    gw = mm(left, right)
    pay_ref[0:samples, :] = mt_right(gb, w)
    pay_ref[samples : samples + width, :] = gw[:, :width] + gw[:, width:]
    rest = gw_out + [jnp.sum(gb, axis=0, keepdims=True), bout]
    base = samples + width
    pay_ref[base : base + 8, :] = jnp.concatenate(rest + [jnp.zeros((2, width), f32)], axis=0)
    pay_ref[base + 8 :, :] = jnp.zeros((pay_ref.shape[0] - base - 8, width), f32)
    p_ex.start()
    pbuf[me_r, :, :] = pay_ref[pl.ds(pl.multiple_of(me_r * part, 8), part), :]
    p_ex.wait_recv()
    total = pbuf[0, :, :]
    for i in range(1, nr):
        total = total + pbuf[i, :, :]
    psum[...] = total
    opay_ref[pl.ds(pl.multiple_of(me_r * part, 8), part), :] = total
    a_ex.start()
    r_ex.wait_recv()
    total = rbuf[0, :, :].astype(f32)
    for i in range(1, ns):
        total = total + rbuf[i, :, :].astype(f32)
    oray_ref[...] = total
    b_ex.wait_recv()
    total = bbuf[0, :, :].astype(f32)
    for i in range(1, nr):
        total = total + bbuf[i, :, :].astype(f32)
    obrick_ref[...] = total
    a_ex.wait_recv()
    x_ex.wait_send()
    for h in range(2):
        s_ex[h].wait_send()
        r_ex.wait_send(h * (ns // 2), ns // 2)
    b_ex.wait_send()
    p_ex.wait_send()
    a_ex.wait_send()


def finish_kernel(color_ref, ray_ref, brick_ref, pay_ref,
                  ocolor_ref, oray_ref, obrick_ref, osample_ref, owh_ref, obh_ref, owo_ref, obo_ref):
    samples, width = osample_ref.shape[1], osample_ref.shape[2]
    base = samples + width
    ocolor_ref[...] = color_ref[...]
    oray_ref[...] = ray_ref[...]
    obrick_ref[0, :, :] = brick_ref[...]
    osample_ref[0, :, :] = pay_ref[0:samples, :]
    owh_ref[0, :, :] = pay_ref[samples:base, :]
    owo_ref[0, :, :] = pay_ref[base : base + 4, :]
    obh_ref[...] = pay_ref[base + 4 : base + 5, :]
    obo_ref[...] = pay_ref[base + 5 : base + 6, 0:4]


def body(ray_code, direction, target, brick_code, sample_code, w_hidden, b_hidden, w_out, b_out, brick_ids, occupancy):
    ns = lax.axis_size("slab")
    nr = lax.axis_size("ray")
    width = ray_code.shape[1]
    rays = direction.shape[0]
    slots = brick_ids.shape[1]
    bricks = brick_code.shape[1]
    samples = sample_code.shape[1]
    positions = slots * samples
    own = rays // ns
    share = bricks // nr
    half = rays // 2
    rows_pay = 256
    part = rows_pay // nr
    vm = pl.BlockSpec(memory_space=pltpu.VMEM)
    sm = pl.BlockSpec(memory_space=pltpu.SMEM)
    sem = lambda *n: pltpu.SemaphoreType.DMA(n)
    shape = jax.ShapeDtypeStruct
    vmem = pltpu.VMEM
    mid = pl.pallas_call(
        functools.partial(step_kernel, ns, nr),
        out_shape=(
            shape((3, own), f32), shape((own, width), f32), shape((share, width), f32), shape((rows_pay, width), f32),
        ),
        in_specs=[vm] * 8 + [sm] + [vm] * 2,
        out_specs=(vm,) * 4,
        scratch_shapes=[
            vmem((rays, width), bf16),
            vmem((slots * rays, width), bf16),
            vmem((slots * rays, width), f32),
            vmem((slots * rays, width), bf16),
            vmem((samples, width), f32),
            vmem((4, samples, 128), f32),
            vmem((32, 8 * width), bf16),
            vmem((4, positions, rays), f32),
            vmem((positions, rays), f32),
            vmem((positions, rays), f32),
            vmem((2, 4, half), f32),
            vmem((2, ns, 4, half), f32),
            vmem((slots * rays // 128, 4 * samples, 128), f32),
            vmem((4 * rays, positions), f32),
            vmem((slots, 4 * rays, width), f32),
            vmem((4 * samples, width), f32),
            vmem((slots * rays, width), f32),
            vmem((rays, width), bf16),
            vmem((bricks, width), bf16),
            vmem((rows_pay, width), f32),
            vmem((ns, own, width), bf16),
            vmem((nr, share, width), bf16),
            vmem((nr, part, width), f32),
            vmem((part, width), f32),
            sem(ns), sem(ns), sem(2, ns), sem(2, ns), sem(ns), sem(ns),
            sem(nr), sem(nr), sem(nr), sem(nr), sem(nr), sem(nr),
        ],
        compiler_params=pltpu.CompilerParams(
            collective_id=0, has_side_effects=True, vmem_limit_bytes=56 * 1024 * 1024
        ),
    )(ray_code, direction[None, :], target, brick_code[0], sample_code[0], w_hidden[0], b_hidden, w_out[0], b_out,
      brick_ids[0], occupancy)
    return pl.pallas_call(
        finish_kernel,
        out_shape=(
            shape((3, own), f32), shape((own, width), f32), shape((1, share, width), f32),
            shape((1, samples, width), f32), shape((1, width, width), f32), shape((1, width), f32),
            shape((1, 4, width), f32), shape((1, 4), f32),
        ),
        in_specs=[vm] * 4,
        out_specs=(vm,) * 8,
    )(*mid)


def solution(mesh):
    in_specs = (
        P(("ray", "slab"), None),
        P("ray"),
        P(None, "ray"),
        P("slab", None, None),
        P("slab", None, None),
        P("slab", None, None),
        P("slab", None),
        P("slab", None, None),
        P("slab", None),
        P("slab", None, "ray"),
        P("slab", "ray"),
    )
    out_specs = (
        P(None, ("ray", "slab")),
        P(("ray", "slab"), None),
        P("slab", "ray", None),
        P("slab", None, None),
        P("slab", None, None),
        P("slab", None),
        P("slab", None, None),
        P("slab", None),
    )
    return jax.shard_map(body, mesh=mesh, in_specs=in_specs, out_specs=out_specs, check_vma=False)
```

```python
import functools
import jax
import jax.numpy as jnp
from jax import lax
from jax.experimental import pallas as pl
from jax.experimental.pallas import tpu as pltpu
from jax.sharding import PartitionSpec as P

step_length = 0.002
f32 = jnp.float32
bf16 = jnp.bfloat16
MESH = pl.DeviceIdType.MESH


def mm(a, b):
    return lax.dot_general(a, b, (((1,), (0,)), ((), ())), preferred_element_type=f32)


def mt(a, b):
    return lax.dot_general(a, b, (((1,), (1,)), ((), ())), preferred_element_type=f32)


def split(x):
    hi = x.astype(bf16)
    return hi, (x - hi.astype(f32)).astype(bf16)


def mm_left(a, x):
    hi, lo = split(x)
    return mm(a, hi) + mm(a, lo)


def mt_right(x, b):
    hi, lo = split(x)
    return mt(hi, b) + mt(lo, b)


def triangle(n, strict_lower):
    row = lax.broadcasted_iota(jnp.int32, (n, n), 0)
    col = lax.broadcasted_iota(jnp.int32, (n, n), 1)
    keep = (row > col) if strict_lower else (row < col)
    return jnp.where(keep, 1.0, 0.0).astype(bf16)


def log1p_small(e):
    series = e * (1.0 - e * (0.5 - e * (1.0 / 3.0 - e * 0.25)))
    return jnp.where(e < 0.01, series, jnp.log(1.0 + e))


def one_minus_exp(o):
    series = o * (1.0 - o * (0.5 - o * (1.0 / 6.0 - o * (1.0 / 24.0))))
    return jnp.where(o < 0.03, series, 1.0 - jnp.exp(-o))


def sigmoid(x):
    return 0.5 * jnp.tanh(0.5 * x) + 0.5


def occupied_mask(occ, samples, positions):
    slot = lax.broadcasted_iota(jnp.int32, (positions, occ.shape[1]), 0) // samples
    return jnp.where(slot < occ, 1.0, 0.0)


def optical_of(raw0, occupied):
    soft = jnp.maximum(raw0, 0.0) + log1p_small(jnp.exp(-jnp.abs(raw0)))
    return step_length * soft * occupied


def torus_offsets(n):
    rows, cols = (4, n // 4) if n % 4 == 0 and n > 8 else (1, n)
    offsets = [(dr, dc) for dr in range(rows) for dc in range(cols) if (dr, dc) != (0, 0)]
    offsets.sort(key=lambda o: -(min(o[0], rows - o[0]) + min(o[1], cols - o[1])))
    return rows, cols, offsets


def peers_of(name, n):
    me = lax.axis_index(name)
    rows, cols, offsets = torus_offsets(n)
    row, col = me // cols, lax.rem(me, cols)
    return [lax.rem(row + dr, rows) * cols + lax.rem(col + dc, cols) for dr, dc in offsets]


def signal_peers(axes):
    barrier = pltpu.get_barrier_semaphore()
    for name, n in axes:
        for peer in peers_of(name, n):
            pl.semaphore_signal(barrier, inc=1, device_id={name: peer}, device_id_type=MESH)


def await_peers(axes):
    pl.semaphore_wait(pltpu.get_barrier_semaphore(), sum(n - 1 for _, n in axes))


class Exchange:
    def __init__(self, name, n, src_of, dst_of, all_of, send, recv):
        self.name, self.n, self.src_of, self.dst_of, self.all_of = name, n, src_of, dst_of, all_of
        self.send, self.recv = send, recv
        self.me = lax.axis_index(name)

    def start(self):
        for peer in peers_of(self.name, self.n):
            pltpu.make_async_remote_copy(
                src_ref=self.src_of(peer), dst_ref=self.dst_of(self.me), send_sem=self.send, recv_sem=self.recv,
                device_id={self.name: peer}, device_id_type=MESH,
            ).start()

    def wait_recv(self):
        pltpu.make_async_copy(self.all_of(self.n - 1), self.all_of(self.n - 1), self.recv).wait()

    def wait_send(self):
        pltpu.make_async_copy(self.all_of(self.n - 1), self.all_of(self.n - 1), self.send).wait()


def step_kernel(ns, nr, x_ref, dir_hbm, target_hbm, brick_hbm, sample_hbm, w_hbm, bh_hbm, wo_hbm, bo_hbm, ids_hbm,
                occ_hbm,
                color_ref, oray_ref, obrick_ref, opay_ref,
                dir_ref, target_ref, brick_ref, sample_ref, w_ref, bh_ref, wo_ref, bo_ref, ids_ref, occ_ref,
                ray_ref, xg_ref, hot_ref, a_ref, abf_ref, nb_ref, corr_ref, left_ref, raw_ref, weight_ref, trail_ref,
                seg_ref, allseg_ref, basis_ref, gj_ref, gr_ref, s_ref, t_ref, ga_ref, gray_ref, gbrick_ref, pay_ref,
                late_ref, rbuf, bbuf, pbuf, psum, pall, lbuf,
                in_sem, xs_send, xs_recv, ss_send, ss_recv, rs_send, rs_recv, bs_send, bs_recv, ps_send, ps_recv,
                ag_send, ag_recv, ls_send, ls_recv):
    slots, rays = ids_ref.shape
    bricks, width = brick_ref.shape
    samples = sample_ref.shape[0]
    positions = slots * samples
    own = rays // ns
    share = bricks // nr
    part = psum.shape[0]
    me = lax.axis_index("slab")
    me_r = lax.axis_index("ray")
    axes = [("slab", ns), ("ray", nr)]

    signal_peers(axes)
    loads = [
        pltpu.make_async_copy(src, dst, in_sem.at[i])
        for i, (src, dst) in enumerate([
            (w_hbm, w_ref), (sample_hbm, sample_ref), (wo_hbm, wo_ref), (bo_hbm, bo_ref), (ids_hbm, ids_ref),
            (brick_hbm, brick_ref), (bh_hbm, bh_ref), (occ_hbm, occ_ref), (dir_hbm, dir_ref),
            (target_hbm, target_ref),
        ])
    ]
    for load in loads:
        load.start()

    def rows(ref, index, size):
        return ref.at[pl.ds(pl.multiple_of(index * size, 8), size), :]

    def first(ref, size):
        return lambda count: ref.at[pl.ds(0, count * size), :]

    def lead(ref):
        return lambda count: ref.at[pl.ds(0, count)]

    x_ex = Exchange("slab", ns, lambda peer: x_ref, lambda slot: rows(ray_ref, slot, own), first(ray_ref, own),
                    xs_send, xs_recv)
    s_ex = Exchange("slab", ns, lambda peer: seg_ref, lambda slot: allseg_ref.at[slot], lead(allseg_ref),
                    ss_send, ss_recv)
    r_ex = Exchange("slab", ns, lambda peer: rows(gray_ref, peer, own), lambda slot: rbuf.at[slot], lead(rbuf),
                    rs_send, rs_recv)
    b_ex = Exchange("ray", nr, lambda peer: rows(gbrick_ref, peer, share), lambda slot: bbuf.at[slot], lead(bbuf),
                    bs_send, bs_recv)
    p_ex = Exchange("ray", nr, lambda peer: rows(pay_ref, peer, part), lambda slot: pbuf.at[slot], lead(pbuf),
                    ps_send, ps_recv)
    a_ex = Exchange("ray", nr, lambda peer: psum, lambda slot: rows(pall, slot, part), first(pall, part),
                    ag_send, ag_recv)
    l_ex = Exchange("ray", nr, lambda peer: late_ref, lambda slot: lbuf.at[slot], lead(lbuf), ls_send, ls_recv)

    for load in loads[:4]:
        load.wait()
    w = w_ref[...]
    w2 = jnp.concatenate([w, w], axis=0)
    nb = -mm(sample_ref[...], w)
    nb_ref[...] = nb
    nbr = nb.astype(bf16).astype(f32)
    wo = wo_ref[...].astype(f32)
    row32 = lax.broadcasted_iota(jnp.int32, (32, width), 0) % 8
    wexp = jnp.concatenate([jnp.broadcast_to(wo[c : c + 1, :], (8, width)) for c in range(4)], axis=0)
    for q in range(8):
        left_ref[:, q * width : (q + 1) * width] = jnp.where(row32 == q, wexp, 0.0).astype(bf16)
    for c in range(4):
        corr_ref[c, :, :] = jnp.broadcast_to(
            bo_ref[0:1, c : c + 1] - jnp.sum(nbr * wo[c : c + 1, :], axis=1, keepdims=True), (samples, 128)
        )
    await_peers(axes)
    x_ex.start()
    ray_ref[pl.ds(pl.multiple_of(me * own, 8), own), :] = x_ref[...]
    for load in loads[4:]:
        load.wait()
    lane = lax.broadcasted_iota(jnp.int32, (128, bricks), 1)
    for k in range(slots):
        for i in range(rays // 128):
            row = ids_ref[k : k + 1, i * 128 : (i + 1) * 128]
            col = jnp.broadcast_to(row, (128, 128)).T
            wide = jnp.concatenate([col] * (bricks // 128), axis=1)
            hot = jnp.where(wide == lane, 1.0, 0.0).astype(bf16)
            at = k * rays + i * 128
            xg_ref[at : at + 128, :] = mm(hot, brick_ref[...]).astype(bf16)
    for bt in range(bricks // 128):
        sub = lax.broadcasted_iota(jnp.int32, (128, rays), 0) + bt * 128
        for k in range(slots):
            hot_ref[bt * 128 : (bt + 1) * 128, k * rays : (k + 1) * rays] = jnp.where(
                ids_ref[k : k + 1, :] == sub, 1.0, 0.0
            ).astype(bf16)
    x_ex.wait_recv()

    for k in range(slots):
        at = k * rays
        both = jnp.concatenate([xg_ref[at : at + rays, :], ray_ref[...]], axis=1)
        a = mm(both, w2) + bh_ref[...]
        a_ref[at : at + rays, :] = a
        abf_ref[at : at + rays, :] = a.astype(bf16)

    def group(g, carry):
        k = g // (samples // 8)
        j0 = pl.multiple_of((g % (samples // 8)) * 8, 8)
        p0 = pl.multiple_of(g * 8, 8)
        nb8 = nb_ref[pl.ds(j0, 8), :].astype(bf16)
        fixes = [corr_ref[c, pl.ds(j0, 8), :] for c in range(4)]
        for rc in range(rays // 256):
            base = pl.multiple_of(k * rays + rc * 256, 256)
            ab = abf_ref[pl.ds(base, 256), :]
            acc = jnp.zeros((32, 256), f32)
            for q in range(0, 8, 2):
                hid = jnp.concatenate(
                    [jnp.maximum(ab, nb8[q : q + 1, :]), jnp.maximum(ab, nb8[q + 1 : q + 2, :])], axis=1
                )
                acc = acc + mt(left_ref[:, q * width : (q + 2) * width], hid)
            for c in range(4):
                raw_ref[c, pl.ds(p0, 8), rc * 256 : (rc + 1) * 256] = acc[c * 8 : (c + 1) * 8, :] + jnp.concatenate(
                    [fixes[c], fixes[c]], axis=1
                )
        return carry

    lax.fori_loop(0, slots * samples // 8, group, 0)

    below = triangle(positions, True)
    above = triangle(positions, False)
    for rc in range(rays // 128):
        cols = slice(rc * 128, (rc + 1) * 128)
        raw0 = raw_ref[0, :, cols]
        occupied = occupied_mask(occ_ref[:, cols], samples, positions)
        optical = optical_of(raw0, occupied)
        entered = mm_left(below, optical)
        weight = jnp.exp(-entered) * one_minus_exp(optical)
        weight_ref[:, cols] = weight
        trail_ref[:, cols] = jnp.exp(-(entered + optical))
        basis_ref[3, :, cols] = step_length * occupied * sigmoid(raw0)
        seg = []
        for c in range(3):
            shade = sigmoid(raw_ref[c + 1, :, cols])
            raw_ref[c + 1, :, cols] = shade
            seg.append(jnp.sum(weight * shade, axis=0, keepdims=True))
        seg.append(jnp.exp(-jnp.sum(optical, axis=0, keepdims=True)))
        seg = jnp.concatenate(seg, axis=0)
        seg_ref[:, cols] = seg
        allseg_ref[me, :, cols] = seg
    s_ex.start()

    col_sums = []
    for rc in range(rays // 128):
        cols = slice(rc * 128, (rc + 1) * 128)
        weight = weight_ref[:, cols]
        trail = trail_ref[:, cols]
        dens = basis_ref[3, :, cols]
        lit = [weight * raw_ref[c + 1, :, cols] for c in range(3)]
        after = mm_left(above, jnp.concatenate(lit, axis=1))
        base = rc * 128 * 8
        sums = []
        parts = []
        for c in range(3):
            shade = raw_ref[c + 1, :, cols]
            u = dens * (shade * trail - after[:, c * 128 : (c + 1) * 128])
            y = lit[c] * (1.0 - shade)
            basis_ref[c, :, cols] = u
            basis_ref[4 + c, :, cols] = y
            parts.append((c, u))
            parts.append((4 + c, y))
        parts.append((3, dens))
        sums = [None] * 7
        for b, value in parts:
            gr_ref[pl.ds(base + b, 128, stride=8), :] = value.T
            sums[b] = jnp.sum(value, axis=0, keepdims=True)
        gr_ref[pl.ds(base + 7, 128, stride=8), :] = jnp.zeros((128, positions), f32)
        col_sums.append(sums)

    lane_p = lax.broadcasted_iota(jnp.int32, (16, positions), 1)

    def ray_group(rg, carry):
        r0 = pl.multiple_of(rg * 8, 8)
        a0 = a_ref[pl.ds(r0, 8), :]
        a1 = a_ref[pl.ds(rays + r0, 8), :]
        for i in range(0, 8, 2):
            halves = []
            for r in (i, i + 1):
                m0 = jnp.where(a0[r : r + 1, :] > nb, 1.0, 0.0).astype(bf16)
                m1 = jnp.where(a1[r : r + 1, :] > nb, 1.0, 0.0).astype(bf16)
                halves.append(jnp.concatenate([m0, m1], axis=0))
            m = jnp.concatenate(halves, axis=1)
            at = pl.multiple_of((r0 + i) * 8, 16)
            g16 = gr_ref[pl.ds(at, 16), :]
            left = jnp.concatenate(
                [jnp.where(lane_p < samples, g16, 0.0), jnp.where(lane_p < samples, 0.0, g16)], axis=0
            ).astype(bf16)
            out = mm(left, m)
            for k in range(2):
                s_ref[k, pl.ds(at, 8), :] = out[k * 16 : k * 16 + 8, :width]
                s_ref[k, pl.ds(pl.multiple_of(at + 8, 8), 8), :] = out[k * 16 + 8 : k * 16 + 16, width:]
        return carry

    lax.fori_loop(0, rays // 8, ray_group, 0)

    s_ex.wait_recv()
    zero3 = jnp.zeros((3, rays), f32)
    one1 = jnp.ones((1, rays), f32)
    ahead = dir_ref[...] == 0

    def low_step(t, state):
        color, trans = state
        piece, through = allseg_ref[t, 0:3, :], allseg_ref[t, 3:4, :]
        color = jnp.where(ahead, color + trans * piece, piece + through * color)
        return color, trans * through

    def high_step(i, state):
        t = ns - 1 - i
        color, trans = state
        piece, through = allseg_ref[t, 0:3, :], allseg_ref[t, 3:4, :]
        color = jnp.where(ahead, piece + through * color, color + trans * piece)
        return color, trans * through

    low_c, low_t = lax.fori_loop(0, me, low_step, (zero3, one1))
    high_c, high_t = lax.fori_loop(0, ns - 1 - me, high_step, (zero3, one1))
    seg_c, seg_t = allseg_ref[me, 0:3, :], allseg_ref[me, 3:4, :]
    before_c = jnp.where(ahead, low_c, high_c)
    before_t = jnp.where(ahead, low_t, high_t)
    after_c = jnp.where(ahead, high_c, low_c)
    color = before_c + before_t * (seg_c + seg_t * after_c)
    residual = color - target_ref[...]
    cot_c = before_t * residual
    tail = before_t * jnp.sum(after_c * residual, axis=0, keepdims=True) * seg_t
    color8 = jnp.concatenate([color, jnp.zeros((5, rays), f32)], axis=0)
    color_ref[...] = pltpu.roll(color8, lax.rem(rays - me * own, rays), 1)[0:3, 0:own]

    lane_row = lax.broadcasted_iota(jnp.int32, (1, width), 1)
    bout = jnp.zeros((1, width), f32)
    gw_out = [jnp.zeros((1, width), f32) for _ in range(4)]
    for rc in range(rays // 128):
        cols = slice(rc * 128, (rc + 1) * 128)
        cots = [cot_c[c : c + 1, cols] for c in range(3)]
        end = tail[:, cols]
        sums = col_sums[rc]
        total0 = cots[0] * sums[0] + cots[1] * sums[1] + cots[2] * sums[2] - end * sums[3]
        bout = bout + jnp.where(lane_row == 0, jnp.sum(total0), 0.0)
        for c in range(3):
            bout = bout + jnp.where(lane_row == c + 1, jnp.sum(cots[c] * sums[4 + c]), 0.0)
        wide = [jnp.broadcast_to(v, (128, 128)).T for v in cots + [end]]
        for k in range(slots):
            take = lambda b: s_ref[k, pl.ds(rc * 1024 + b, 128, stride=8), :]
            s_all = [wide[0] * take(0) + wide[1] * take(1) + wide[2] * take(2) - wide[3] * take(3)]
            s_all += [wide[c] * take(4 + c) for c in range(3)]
            at = k * rays + rc * 128
            a = a_ref[at : at + 128, :]
            ga = jnp.zeros((128, width), f32)
            for c in range(4):
                ga = ga + s_all[c] * wo[c : c + 1, :]
                gw_out[c] = gw_out[c] + jnp.sum(s_all[c] * a, axis=0, keepdims=True)
            ga_ref[at : at + 128, :] = ga
    ga_sum = ga_ref[0:rays, :] + ga_ref[rays:, :]
    gray_ref[...] = mt_right(ga_sum, w).astype(bf16)
    r_ex.start()
    rbuf[me, :, :] = gray_ref[pl.ds(pl.multiple_of(me * own, 8), own), :]

    ga_all = jnp.concatenate(split(ga_ref[...]), axis=1)
    gbp = []
    for bt in range(bricks // 128):
        pre = mm(hot_ref[bt * 128 : (bt + 1) * 128, :], ga_all)
        pre = pre[:, :width] + pre[:, width:]
        gbp.append(pre)
        gbrick_ref[bt * 128 : (bt + 1) * 128, :] = mt_right(pre, w).astype(bf16)
    b_ex.start()
    bbuf[me_r, :, :] = gbrick_ref[pl.ds(pl.multiple_of(me_r * share, 8), share), :]

    right = jnp.concatenate(gbp + [ga_sum], axis=0)
    right = jnp.concatenate(split(right), axis=1)
    left = jnp.concatenate([brick_ref[...], ray_ref[...]], axis=0).astype(f32).T.astype(bf16)
    gw = mm(left, right)
    pay_ref[...] = gw[:, :width] + gw[:, width:]
    p_ex.start()
    pbuf[me_r, :, :] = pay_ref[pl.ds(pl.multiple_of(me_r * part, 8), part), :]

    for rc in range(rays // 128):
        cols = slice(rc * 128, (rc + 1) * 128)
        cots = [cot_c[c : c + 1, cols] for c in range(3)]
        grads = [-tail[:, cols] * basis_ref[3, :, cols]]
        for c in range(3):
            grads[0] = grads[0] + cots[c] * basis_ref[c, :, cols]
            grads.append(cots[c] * basis_ref[4 + c, :, cols])
        for c in range(4):
            for k in range(slots):
                gj_ref[k * (rays // 128) + rc, pl.ds(c, samples, stride=4), :] = grads[c][
                    k * samples : (k + 1) * samples, :
                ]

    sub8 = lax.broadcasted_iota(jnp.int32, (8, width), 0)
    one, zero = jnp.ones((), bf16), jnp.zeros((), bf16)

    def sample_pair(jp, carry):
        row8 = pl.multiple_of(jp * 8, 8)
        n0 = nb_ref[pl.ds(jp * 2, 1), :].astype(bf16)
        n1 = nb_ref[pl.ds(jp * 2 + 1, 1), :].astype(bf16)
        acc = jnp.zeros((8, 2 * width), f32)
        for i in range(slots * rays // 256):
            a = abf_ref[i * 256 : (i + 1) * 256, :]
            m = jnp.concatenate([jnp.where(a > n0, one, zero), jnp.where(a > n1, one, zero)], axis=1)
            left = jnp.concatenate([gj_ref[2 * i, pl.ds(row8, 8), :], gj_ref[2 * i + 1, pl.ds(row8, 8), :]], axis=1)
            acc = acc + mm(left.astype(bf16), m)
        t_ref[pl.ds(row8, 8), :] = jnp.where(sub8 < 4, acc[:, :width], acc[:, width:])
        return carry

    lax.fori_loop(0, samples // 2, sample_pair, 0)

    gb = jnp.zeros((samples, width), f32)
    for c in range(4):
        t_c = t_ref[pl.ds(c, samples, stride=4), :]
        gb = gb + t_c * wo[c : c + 1, :]
        gw_out[c] = gw_out[c] - jnp.sum(t_c * nb, axis=0, keepdims=True)
    small = jnp.concatenate(gw_out + [jnp.sum(gb, axis=0, keepdims=True), bout, jnp.zeros((2, width), f32)], axis=0)
    late_ref[...] = jnp.concatenate([gb.astype(bf16)] + [v for v in split(small)], axis=0)
    l_ex.start()
    lbuf[me_r, :, :] = late_ref[...]
    p_ex.wait_recv()
    total = pbuf[0, :, :]
    for i in range(1, nr):
        total = total + pbuf[i, :, :]
    psum[...] = total
    pall[pl.ds(pl.multiple_of(me_r * part, 8), part), :] = total
    a_ex.start()
    b_ex.wait_recv()
    total = bbuf[0, :, :].astype(f32)
    for i in range(1, nr):
        total = total + bbuf[i, :, :].astype(f32)
    obrick_ref[...] = total
    r_ex.wait_recv()
    total = rbuf[0, :, :].astype(f32)
    for i in range(1, ns):
        total = total + rbuf[i, :, :].astype(f32)
    oray_ref[...] = total
    x_ex.wait_send()
    s_ex.wait_send()
    r_ex.wait_send()
    b_ex.wait_send()
    p_ex.wait_send()
    l_ex.wait_recv()
    total = lbuf[0, :, :].astype(f32)
    for i in range(1, nr):
        total = total + lbuf[i, :, :].astype(f32)
    gb = total[0:samples, :]
    opay_ref[0:samples, :] = mt_right(gb, w)
    opay_ref[samples + width :, :] = total[samples : samples + 8, :] + total[samples + 8 :, :]
    extra = mm_left(sample_ref[...].astype(f32).T.astype(bf16), gb)
    a_ex.wait_recv()
    opay_ref[samples : samples + width, :] = pall[...] + extra
    a_ex.wait_send()
    l_ex.wait_send()


def finish_kernel(color_ref, ray_ref, brick_ref, pay_ref,
                  ocolor_ref, oray_ref, obrick_ref, osample_ref, owh_ref, obh_ref, owo_ref, obo_ref):
    samples, width = osample_ref.shape[1], osample_ref.shape[2]
    base = samples + width
    ocolor_ref[...] = color_ref[...]
    oray_ref[...] = ray_ref[...]
    obrick_ref[0, :, :] = brick_ref[...]
    osample_ref[0, :, :] = pay_ref[0:samples, :]
    owh_ref[0, :, :] = pay_ref[samples:base, :]
    owo_ref[0, :, :] = pay_ref[base : base + 4, :]
    obh_ref[...] = pay_ref[base + 4 : base + 5, :]
    obo_ref[...] = pay_ref[base + 5 : base + 6, 0:4]


def body(ray_code, direction, target, brick_code, sample_code, w_hidden, b_hidden, w_out, b_out, brick_ids, occupancy):
    ns = lax.axis_size("slab")
    nr = lax.axis_size("ray")
    width = ray_code.shape[1]
    rays = direction.shape[0]
    slots = brick_ids.shape[1]
    bricks = brick_code.shape[1]
    samples = sample_code.shape[1]
    positions = slots * samples
    own = rays // ns
    share = bricks // nr
    part = width // nr
    late = samples + 16
    rows_pay = samples + width + 8
    vm = pl.BlockSpec(memory_space=pltpu.VMEM)
    anywhere = pl.BlockSpec(memory_space=pl.ANY)
    sem = pltpu.SemaphoreType.DMA
    shape = jax.ShapeDtypeStruct
    vmem = pltpu.VMEM
    ins = (direction[None, :], target, brick_code[0], sample_code[0], w_hidden[0], b_hidden, w_out[0], b_out,
           brick_ids[0], occupancy)
    mid = pl.pallas_call(
        functools.partial(step_kernel, ns, nr),
        out_shape=(
            shape((3, own), f32), shape((own, width), f32), shape((share, width), f32), shape((rows_pay, width), f32),
        ),
        in_specs=[vm] + [anywhere] * len(ins),
        out_specs=(vm,) * 4,
        scratch_shapes=[vmem(v.shape, v.dtype) for v in ins] + [
            vmem((rays, width), bf16),
            vmem((slots * rays, width), bf16),
            vmem((bricks, slots * rays), bf16),
            vmem((slots * rays, width), f32),
            vmem((slots * rays, width), bf16),
            vmem((samples, width), f32),
            vmem((4, samples, 128), f32),
            vmem((32, 8 * width), bf16),
            vmem((4, positions, rays), f32),
            vmem((positions, rays), f32),
            vmem((positions, rays), f32),
            vmem((4, rays), f32),
            vmem((ns, 4, rays), f32),
            vmem((7, positions, rays), f32),
            vmem((slots * rays // 128, 4 * samples, 128), f32),
            vmem((8 * rays, positions), f32),
            vmem((slots, 8 * rays, width), f32),
            vmem((4 * samples, width), f32),
            vmem((slots * rays, width), f32),
            vmem((rays, width), bf16),
            vmem((bricks, width), bf16),
            vmem((width, width), f32),
            vmem((late, width), bf16),
            vmem((ns, own, width), bf16),
            vmem((nr, share, width), bf16),
            vmem((nr, part, width), f32),
            vmem((part, width), f32),
            vmem((width, width), f32),
            vmem((nr, late, width), bf16),
            sem((len(ins),)), sem, sem, sem, sem, sem, sem, sem, sem, sem, sem, sem, sem, sem, sem,
        ],
        compiler_params=pltpu.CompilerParams(
            collective_id=0, has_side_effects=True, vmem_limit_bytes=56 * 1024 * 1024
        ),
    )(ray_code, *ins)
    return pl.pallas_call(
        finish_kernel,
        out_shape=(
            shape((3, own), f32), shape((own, width), f32), shape((1, share, width), f32),
            shape((1, samples, width), f32), shape((1, width, width), f32), shape((1, width), f32),
            shape((1, 4, width), f32), shape((1, 4), f32),
        ),
        in_specs=[vm] * 4,
        out_specs=(vm,) * 8,
    )(*mid)


def solution(mesh):
    in_specs = (
        P(("ray", "slab"), None),
        P("ray"),
        P(None, "ray"),
        P("slab", None, None),
        P("slab", None, None),
        P("slab", None, None),
        P("slab", None),
        P("slab", None, None),
        P("slab", None),
        P("slab", None, "ray"),
        P("slab", "ray"),
    )
    out_specs = (
        P(None, ("ray", "slab")),
        P(("ray", "slab"), None),
        P("slab", "ray", None),
        P("slab", None, None),
        P("slab", None, None),
        P("slab", None),
        P("slab", None, None),
        P("slab", None),
    )
    return jax.shard_map(body, mesh=mesh, in_specs=in_specs, out_specs=out_specs, check_vma=False)
```

```python
import functools
import jax
import jax.numpy as jnp
from jax import lax
from jax.experimental import pallas as pl
from jax.experimental.pallas import tpu as pltpu
from jax.sharding import PartitionSpec as P

step_length = 0.002
f32 = jnp.float32
bf16 = jnp.bfloat16
MESH = pl.DeviceIdType.MESH


def mm(a, b):
    return lax.dot_general(a, b, (((1,), (0,)), ((), ())), preferred_element_type=f32)


def mt(a, b):
    return lax.dot_general(a, b, (((1,), (1,)), ((), ())), preferred_element_type=f32)


def split(x):
    hi = x.astype(bf16)
    return hi, (x - hi.astype(f32)).astype(bf16)


def mm_left(a, x):
    hi, lo = split(x)
    return mm(a, hi) + mm(a, lo)


def mt_right(x, b):
    hi, lo = split(x)
    return mt(hi, b) + mt(lo, b)


def triangle(n, strict_lower):
    row = lax.broadcasted_iota(jnp.int32, (n, n), 0)
    col = lax.broadcasted_iota(jnp.int32, (n, n), 1)
    keep = (row > col) if strict_lower else (row < col)
    return jnp.where(keep, 1.0, 0.0).astype(bf16)


def log1p_small(e):
    series = e * (1.0 - e * (0.5 - e * (1.0 / 3.0 - e * 0.25)))
    return jnp.where(e < 0.01, series, jnp.log(1.0 + e))


def one_minus_exp(o):
    series = o * (1.0 - o * (0.5 - o * (1.0 / 6.0 - o * (1.0 / 24.0))))
    return jnp.where(o < 0.03, series, 1.0 - jnp.exp(-o))


def sigmoid(x):
    return 0.5 * jnp.tanh(0.5 * x) + 0.5


def occupied_mask(occ, samples, positions):
    slot = lax.broadcasted_iota(jnp.int32, (positions, occ.shape[1]), 0) // samples
    return jnp.where(slot < occ, 1.0, 0.0)


def optical_of(raw0, occupied):
    soft = jnp.maximum(raw0, 0.0) + log1p_small(jnp.exp(-jnp.abs(raw0)))
    return step_length * soft * occupied


def torus_offsets(n):
    rows, cols = (4, n // 4) if n % 4 == 0 and n > 8 else (1, n)
    offsets = [(dr, dc) for dr in range(rows) for dc in range(cols) if (dr, dc) != (0, 0)]
    offsets.sort(key=lambda o: -(min(o[0], rows - o[0]) + min(o[1], cols - o[1])))
    return rows, cols, offsets


def peers_of(name, n):
    me = lax.axis_index(name)
    rows, cols, offsets = torus_offsets(n)
    row, col = me // cols, lax.rem(me, cols)
    return [lax.rem(row + dr, rows) * cols + lax.rem(col + dc, cols) for dr, dc in offsets]


def signal_peers(axes):
    barrier = pltpu.get_barrier_semaphore()
    for name, n in axes:
        for peer in peers_of(name, n):
            pl.semaphore_signal(barrier, inc=1, device_id={name: peer}, device_id_type=MESH)


def await_peers(axes):
    pl.semaphore_wait(pltpu.get_barrier_semaphore(), sum(n - 1 for _, n in axes))


class Exchange:
    def __init__(self, name, n, src_of, dst_of, all_of, send, recv):
        self.name, self.n, self.src_of, self.dst_of, self.all_of = name, n, src_of, dst_of, all_of
        self.send, self.recv = send, recv
        self.me = lax.axis_index(name)

    def start(self):
        for peer in peers_of(self.name, self.n):
            pltpu.make_async_remote_copy(
                src_ref=self.src_of(peer), dst_ref=self.dst_of(self.me), send_sem=self.send, recv_sem=self.recv,
                device_id={self.name: peer}, device_id_type=MESH,
            ).start()

    def wait_recv(self):
        pltpu.make_async_copy(self.all_of(self.n - 1), self.all_of(self.n - 1), self.recv).wait()

    def wait_send(self):
        pltpu.make_async_copy(self.all_of(self.n - 1), self.all_of(self.n - 1), self.send).wait()


def step_kernel(ns, nr, x_ref, dir_hbm, target_hbm, brick_hbm, sample_hbm, w_hbm, bh_hbm, wo_hbm, bo_hbm, ids_hbm,
                occ_hbm,
                color_ref, oray_ref, obrick_ref, opay_ref,
                dir_ref, target_ref, brick_ref, sample_ref, w_ref, bh_ref, wo_ref, bo_ref, ids_ref, occ_ref,
                ray_ref, xg_ref, hot_ref, wide_ref, bt_ref, st_ref, abt_ref, a_ref, nb_ref, corr_ref, left_ref, raw_ref, weight_ref, trail_ref,
                seg_ref, allseg_ref, basis_ref, gj_ref, gr_ref, s_ref, t_ref, ga_ref, gray_ref, gbrick_ref, pay_ref,
                late_ref, early_ref, rbuf, bbuf, pbuf, psum, pall, lbuf, ebuf,
                in_sem, xs_send, xs_recv, ss_send, ss_recv, rs_send, rs_recv, bs_send, bs_recv, ps_send, ps_recv,
                ag_send, ag_recv, ls_send, ls_recv, es_send, es_recv):
    slots, rays = ids_ref.shape
    bricks, width = brick_ref.shape
    samples = sample_ref.shape[0]
    positions = slots * samples
    own = rays // ns
    share = bricks // nr
    part = psum.shape[0]
    me = lax.axis_index("slab")
    me_r = lax.axis_index("ray")
    axes = [("slab", ns), ("ray", nr)]

    signal_peers(axes)
    loads = [
        pltpu.make_async_copy(src, dst, in_sem.at[i])
        for i, (src, dst) in enumerate([
            (w_hbm, w_ref), (sample_hbm, sample_ref), (wo_hbm, wo_ref), (bo_hbm, bo_ref), (ids_hbm, ids_ref),
            (brick_hbm, brick_ref), (bh_hbm, bh_ref), (occ_hbm, occ_ref), (dir_hbm, dir_ref),
            (target_hbm, target_ref),
        ])
    ]
    for load in loads:
        load.start()

    def rows(ref, index, size):
        return ref.at[pl.ds(pl.multiple_of(index * size, 8), size), :]

    def first(ref, size):
        return lambda count: ref.at[pl.ds(0, count * size), :]

    def lead(ref):
        return lambda count: ref.at[pl.ds(0, count)]

    x_ex = Exchange("slab", ns, lambda peer: x_ref, lambda slot: rows(ray_ref, slot, own), first(ray_ref, own),
                    xs_send, xs_recv)
    s_ex = Exchange("slab", ns, lambda peer: seg_ref, lambda slot: allseg_ref.at[slot], lead(allseg_ref),
                    ss_send, ss_recv)
    r_ex = Exchange("slab", ns, lambda peer: rows(gray_ref, peer, own), lambda slot: rbuf.at[slot], lead(rbuf),
                    rs_send, rs_recv)
    b_ex = Exchange("ray", nr, lambda peer: rows(gbrick_ref, peer, share), lambda slot: bbuf.at[slot], lead(bbuf),
                    bs_send, bs_recv)
    p_ex = Exchange("ray", nr, lambda peer: rows(pay_ref, peer, part), lambda slot: pbuf.at[slot], lead(pbuf),
                    ps_send, ps_recv)
    a_ex = Exchange("ray", nr, lambda peer: psum, lambda slot: rows(pall, slot, part), first(pall, part),
                    ag_send, ag_recv)
    l_ex = Exchange("ray", nr, lambda peer: late_ref, lambda slot: lbuf.at[slot], lead(lbuf), ls_send, ls_recv)
    e_ex = Exchange("ray", nr, lambda peer: early_ref, lambda slot: ebuf.at[slot], lead(ebuf), es_send, es_recv)

    await_peers(axes)
    x_ex.start()
    ray_ref[pl.ds(pl.multiple_of(me * own, 8), own), :] = x_ref[...]
    for load in loads[:4]:
        load.wait()
    w = w_ref[...]
    w2 = jnp.concatenate([w, w], axis=0)
    nb = -mm(sample_ref[...], w)
    nb_ref[...] = nb
    nbr = nb.astype(bf16).astype(f32)
    wo = wo_ref[...].astype(f32)
    row32 = lax.broadcasted_iota(jnp.int32, (32, width), 0) % 8
    wexp = jnp.concatenate([jnp.broadcast_to(wo[c : c + 1, :], (8, width)) for c in range(4)], axis=0)
    for q in range(8):
        left_ref[:, q * width : (q + 1) * width] = jnp.where(row32 == q, wexp, 0.0).astype(bf16)
    for c in range(4):
        corr_ref[c, :, :] = jnp.broadcast_to(
            bo_ref[0:1, c : c + 1] - jnp.sum(nbr * wo[c : c + 1, :], axis=1, keepdims=True), (samples, 128)
        )
    for load in loads[4:]:
        load.wait()
    nbt = nb.T.astype(bf16)
    pick = lax.broadcasted_iota(jnp.int32, (samples, 256), 0)
    side = lax.broadcasted_iota(jnp.int32, (samples, 256), 1) // 128
    for j in range(0, samples, 2):
        wide_ref[:, j * 128 : (j + 2) * 128] = mm(
            nbt, jnp.where(pick == side + j, 1.0, 0.0).astype(bf16)
        ).astype(bf16)
    wt = jnp.concatenate([w.astype(f32).T.astype(bf16)] * 2, axis=1)
    bias = jnp.broadcast_to(bh_ref[...], (128, width)).T
    bias = jnp.concatenate([bias] * (rays // 128), axis=1)
    bt_ref[...] = brick_ref[...].astype(f32).T.astype(bf16)
    st_ref[...] = sample_ref[...].astype(f32).T.astype(bf16)
    lane = lax.broadcasted_iota(jnp.int32, (128, bricks), 1)
    for k in range(slots):
        for i in range(rays // 128):
            row = ids_ref[k : k + 1, i * 128 : (i + 1) * 128]
            col = jnp.broadcast_to(row, (128, 128)).T
            wide = jnp.concatenate([col] * (bricks // 128), axis=1)
            hot = jnp.where(wide == lane, 1.0, 0.0).astype(bf16)
            at = k * rays + i * 128
            xg_ref[at : at + 128, :] = mm(hot, brick_ref[...]).astype(bf16)
    for bt in range(bricks // 128):
        sub = lax.broadcasted_iota(jnp.int32, (128, rays), 0) + bt * 128
        for k in range(slots):
            hot_ref[bt * 128 : (bt + 1) * 128, k * rays : (k + 1) * rays] = jnp.where(
                ids_ref[k : k + 1, :] == sub, 1.0, 0.0
            ).astype(bf16)
    x_ex.wait_recv()

    for k in range(slots):
        at = k * rays
        both = jnp.concatenate([xg_ref[at : at + rays, :], ray_ref[...]], axis=1)
        a = mm(both, w2) + bh_ref[...]
        a_ref[at : at + rays, :] = a
        abt_ref[k, :, :] = (mt(wt, both) + bias).astype(bf16)

    def group(g, carry):
        k = g // (samples // 8)
        j0 = pl.multiple_of((g % (samples // 8)) * 8, 8)
        p0 = pl.multiple_of(g * 8, 8)
        fixes = [corr_ref[c, pl.ds(j0, 8), :] for c in range(4)]
        for rc in range(rays // 256):
            ab = abt_ref[k, :, rc * 256 : (rc + 1) * 256]
            acc = jnp.zeros((32, 256), f32)
            for q in range(0, 8, 2):
                parts = []
                for d in range(2):
                    n = wide_ref[:, pl.ds(pl.multiple_of((j0 + q + d) * 128, 128), 128)]
                    parts.append(jnp.maximum(ab, jnp.concatenate([n, n], axis=1)))
                acc = acc + mm(left_ref[:, q * width : (q + 2) * width], jnp.concatenate(parts, axis=0))
            for c in range(4):
                raw_ref[c, pl.ds(p0, 8), rc * 256 : (rc + 1) * 256] = acc[c * 8 : (c + 1) * 8, :] + jnp.concatenate(
                    [fixes[c], fixes[c]], axis=1
                )
        return carry

    lax.fori_loop(0, slots * samples // 8, group, 0)

    below = triangle(positions, True)
    above = triangle(positions, False)
    for rc in range(rays // 128):
        cols = slice(rc * 128, (rc + 1) * 128)
        raw0 = raw_ref[0, :, cols]
        occupied = occupied_mask(occ_ref[:, cols], samples, positions)
        optical = optical_of(raw0, occupied)
        entered = mm_left(below, optical)
        weight = jnp.exp(-entered) * one_minus_exp(optical)
        weight_ref[:, cols] = weight
        trail_ref[:, cols] = jnp.exp(-(entered + optical))
        basis_ref[3, :, cols] = step_length * occupied * sigmoid(raw0)
        seg = []
        for c in range(3):
            shade = sigmoid(raw_ref[c + 1, :, cols])
            raw_ref[c + 1, :, cols] = shade
            seg.append(jnp.sum(weight * shade, axis=0, keepdims=True))
        seg.append(jnp.exp(-jnp.sum(optical, axis=0, keepdims=True)))
        seg = jnp.concatenate(seg, axis=0)
        seg_ref[:, cols] = seg
        allseg_ref[me, :, cols] = seg
    s_ex.start()

    col_sums = []
    all_levels = []
    ends = []
    for rc in range(rays // 128):
        cols = slice(rc * 128, (rc + 1) * 128)
        weight = weight_ref[:, cols]
        trail = trail_ref[:, cols]
        dens = basis_ref[3, :, cols]
        lit = [weight * raw_ref[c + 1, :, cols] for c in range(3)]
        after = mm_left(above, jnp.concatenate(lit, axis=1))
        base = rc * 128 * 8
        levels = []
        parts = []
        for c in range(3):
            shade = raw_ref[c + 1, :, cols]
            u = shade * trail - after[:, c * 128 : (c + 1) * 128]
            level = jnp.mean(u, axis=0, keepdims=True)
            levels.append(level)
            u = dens * (u - level)
            y = lit[c] * (1.0 - shade)
            basis_ref[c, :, cols] = u
            basis_ref[4 + c, :, cols] = y
            parts.append((c, u))
            parts.append((4 + c, y))
        parts.append((3, dens))
        sums = [None] * 7
        for b, value in parts:
            gr_ref[pl.ds(base + b, 128, stride=8), :] = value.T
            sums[b] = jnp.sum(value, axis=0, keepdims=True)
        gr_ref[pl.ds(base + 7, 128, stride=8), :] = jnp.zeros((128, positions), f32)
        col_sums.append(sums)
        all_levels.append(levels)

    lane_p = lax.broadcasted_iota(jnp.int32, (16, positions), 1)

    def ray_group(rg, carry):
        r0 = pl.multiple_of(rg * 8, 8)
        a0 = a_ref[pl.ds(r0, 8), :]
        a1 = a_ref[pl.ds(rays + r0, 8), :]
        for i in range(0, 8, 2):
            halves = []
            for r in (i, i + 1):
                m0 = jnp.where(a0[r : r + 1, :] > nb, 1.0, 0.0).astype(bf16)
                m1 = jnp.where(a1[r : r + 1, :] > nb, 1.0, 0.0).astype(bf16)
                halves.append(jnp.concatenate([m0, m1], axis=0))
            m = jnp.concatenate(halves, axis=1)
            at = pl.multiple_of((r0 + i) * 8, 16)
            g16 = gr_ref[pl.ds(at, 16), :]
            left = jnp.concatenate(
                [jnp.where(lane_p < samples, g16, 0.0), jnp.where(lane_p < samples, 0.0, g16)], axis=0
            ).astype(bf16)
            out = mm(left, m)
            for k in range(2):
                s_ref[k, pl.ds(at, 8), :] = out[k * 16 : k * 16 + 8, :width]
                s_ref[k, pl.ds(pl.multiple_of(at + 8, 8), 8), :] = out[k * 16 + 8 : k * 16 + 16, width:]
        return carry

    lax.fori_loop(0, rays // 8, ray_group, 0)

    s_ex.wait_recv()
    zero3 = jnp.zeros((3, rays), f32)
    one1 = jnp.ones((1, rays), f32)
    ahead = dir_ref[...] == 0

    def low_step(t, state):
        color, trans = state
        piece, through = allseg_ref[t, 0:3, :], allseg_ref[t, 3:4, :]
        color = jnp.where(ahead, color + trans * piece, piece + through * color)
        return color, trans * through

    def high_step(i, state):
        t = ns - 1 - i
        color, trans = state
        piece, through = allseg_ref[t, 0:3, :], allseg_ref[t, 3:4, :]
        color = jnp.where(ahead, piece + through * color, color + trans * piece)
        return color, trans * through

    low_c, low_t = lax.fori_loop(0, me, low_step, (zero3, one1))
    high_c, high_t = lax.fori_loop(0, ns - 1 - me, high_step, (zero3, one1))
    seg_c, seg_t = allseg_ref[me, 0:3, :], allseg_ref[me, 3:4, :]
    before_c = jnp.where(ahead, low_c, high_c)
    before_t = jnp.where(ahead, low_t, high_t)
    after_c = jnp.where(ahead, high_c, low_c)
    color = before_c + before_t * (seg_c + seg_t * after_c)
    residual = color - target_ref[...]
    cot_c = before_t * residual
    tail = before_t * jnp.sum(after_c * residual, axis=0, keepdims=True) * seg_t
    color8 = jnp.concatenate([color, jnp.zeros((5, rays), f32)], axis=0)
    color_ref[...] = pltpu.roll(color8, lax.rem(rays - me * own, rays), 1)[0:3, 0:own]

    lane_row = lax.broadcasted_iota(jnp.int32, (1, width), 1)
    bout = jnp.zeros((1, width), f32)
    gw_out = [jnp.zeros((1, width), f32) for _ in range(4)]
    for rc in range(rays // 128):
        cols = slice(rc * 128, (rc + 1) * 128)
        cots = [cot_c[c : c + 1, cols] for c in range(3)]
        end = tail[:, cols]
        for c in range(3):
            end = end - cots[c] * all_levels[rc][c]
        ends.append(end)
        sums = col_sums[rc]
        total0 = cots[0] * sums[0] + cots[1] * sums[1] + cots[2] * sums[2] - end * sums[3]
        bout = bout + jnp.where(lane_row == 0, jnp.sum(total0), 0.0)
        for c in range(3):
            bout = bout + jnp.where(lane_row == c + 1, jnp.sum(cots[c] * sums[4 + c]), 0.0)
        wide = [jnp.broadcast_to(v, (128, 128)).T for v in cots + [end]]
        for k in range(slots):
            take = lambda b: s_ref[k, pl.ds(rc * 1024 + b, 128, stride=8), :]
            s_all = [wide[0] * take(0) + wide[1] * take(1) + wide[2] * take(2) - wide[3] * take(3)]
            s_all += [wide[c] * take(4 + c) for c in range(3)]
            at = k * rays + rc * 128
            a = a_ref[at : at + 128, :]
            ga = jnp.zeros((128, width), f32)
            for c in range(4):
                ga = ga + s_all[c] * wo[c : c + 1, :]
                gw_out[c] = gw_out[c] + jnp.sum(s_all[c] * a, axis=0, keepdims=True)
            ga_ref[at : at + 128, :] = ga
    ga_sum = ga_ref[0:rays, :] + ga_ref[rays:, :]
    gray_ref[...] = mt_right(ga_sum, w).astype(bf16)
    r_ex.start()
    rbuf[me, :, :] = gray_ref[pl.ds(pl.multiple_of(me * own, 8), own), :]

    ga_all = jnp.concatenate(split(ga_ref[...]), axis=1)
    gbp = []
    for bt in range(bricks // 128):
        pre = mm(hot_ref[bt * 128 : (bt + 1) * 128, :], ga_all)
        pre = pre[:, :width] + pre[:, width:]
        gbp.append(pre)
        gbrick_ref[bt * 128 : (bt + 1) * 128, :] = mt_right(pre, w).astype(bf16)
    b_ex.start()
    bbuf[me_r, :, :] = gbrick_ref[pl.ds(pl.multiple_of(me_r * share, 8), share), :]

    right = jnp.concatenate(gbp + [ga_sum], axis=0)
    right = jnp.concatenate(split(right), axis=1)
    left = jnp.concatenate([bt_ref[...], ray_ref[...].astype(f32).T.astype(bf16)], axis=1)
    gw = mm(left, right)
    pay_ref[...] = gw[:, :width] + gw[:, width:]
    p_ex.start()
    pbuf[me_r, :, :] = pay_ref[pl.ds(pl.multiple_of(me_r * part, 8), part), :]

    for rc in range(rays // 128):
        cols = slice(rc * 128, (rc + 1) * 128)
        cots = [cot_c[c : c + 1, cols] for c in range(3)]
        grads = [-ends[rc] * basis_ref[3, :, cols]]
        for c in range(3):
            grads[0] = grads[0] + cots[c] * basis_ref[c, :, cols]
            grads.append(cots[c] * basis_ref[4 + c, :, cols])
        for c in range(4):
            for k in range(slots):
                gj_ref[k * (rays // 128) + rc, pl.ds(c, samples, stride=4), :] = grads[c][
                    k * samples : (k + 1) * samples, :
                ]

    sub8 = lax.broadcasted_iota(jnp.int32, (8, width), 0)

    def sample_pair(jp, carry):
        row8 = pl.multiple_of(jp * 8, 8)
        n0 = nb_ref[pl.ds(jp * 2, 1), :]
        n1 = nb_ref[pl.ds(jp * 2 + 1, 1), :]
        acc = jnp.zeros((8, 2 * width), f32)
        for i in range(slots * rays // 256):
            a = a_ref[i * 256 : (i + 1) * 256, :]
            m = jnp.concatenate(
                [jnp.where(a > n0, 1.0, 0.0).astype(bf16), jnp.where(a > n1, 1.0, 0.0).astype(bf16)], axis=1
            )
            left = jnp.concatenate([gj_ref[2 * i, pl.ds(row8, 8), :], gj_ref[2 * i + 1, pl.ds(row8, 8), :]], axis=1)
            acc = acc + mm(left.astype(bf16), m)
        t_ref[pl.ds(row8, 8), :] = jnp.where(sub8 < 4, acc[:, :width], acc[:, width:])
        return carry

    gb_sum = jnp.zeros((1, width), f32)
    mid = samples // 2
    for h in range(2):
        lax.fori_loop(h * mid // 2, (h + 1) * mid // 2, sample_pair, 0)
        gb = jnp.zeros((mid, width), f32)
        for c in range(4):
            t_c = t_ref[pl.ds(h * mid * 4 + c, mid, stride=4), :]
            gb = gb + t_c * wo[c : c + 1, :]
            gw_out[c] = gw_out[c] - jnp.sum(t_c * nb[h * mid : (h + 1) * mid, :], axis=0, keepdims=True)
        gb_sum = gb_sum + jnp.sum(gb, axis=0, keepdims=True)
        if h == 0:
            early_ref[...] = gb.astype(bf16)
            e_ex.start()
            ebuf[me_r, :, :] = early_ref[...]
        else:
            small = jnp.concatenate(gw_out + [gb_sum, bout, jnp.zeros((2, width), f32)], axis=0)
            late_ref[...] = jnp.concatenate([gb.astype(bf16)] + [v for v in split(small)], axis=0)
            l_ex.start()
            lbuf[me_r, :, :] = late_ref[...]
    p_ex.wait_recv()
    total = pbuf[0, :, :]
    for i in range(1, nr):
        total = total + pbuf[i, :, :]
    psum[...] = total
    pall[pl.ds(pl.multiple_of(me_r * part, 8), part), :] = total
    a_ex.start()
    b_ex.wait_recv()
    total = bbuf[0, :, :].astype(f32)
    for i in range(1, nr):
        total = total + bbuf[i, :, :].astype(f32)
    obrick_ref[...] = total
    r_ex.wait_recv()
    total = rbuf[0, :, :].astype(f32)
    for i in range(1, ns):
        total = total + rbuf[i, :, :].astype(f32)
    oray_ref[...] = total
    x_ex.wait_send()
    s_ex.wait_send()
    r_ex.wait_send()
    b_ex.wait_send()
    p_ex.wait_send()
    e_ex.wait_recv()
    l_ex.wait_recv()
    front = ebuf[0, :, :].astype(f32)
    total = lbuf[0, :, :].astype(f32)
    for i in range(1, nr):
        front = front + ebuf[i, :, :].astype(f32)
        total = total + lbuf[i, :, :].astype(f32)
    gb = jnp.concatenate([front, total[0:mid, :]], axis=0)
    opay_ref[0:samples, :] = mt_right(gb, w)
    opay_ref[samples + width :, :] = total[mid : mid + 8, :] + total[mid + 8 :, :]
    extra = mm_left(st_ref[...], gb)
    a_ex.wait_recv()
    opay_ref[samples : samples + width, :] = pall[...] + extra
    a_ex.wait_send()
    e_ex.wait_send()
    l_ex.wait_send()


def finish_kernel(color_ref, ray_ref, brick_ref, pay_ref,
                  ocolor_ref, oray_ref, obrick_ref, osample_ref, owh_ref, obh_ref, owo_ref, obo_ref):
    samples, width = osample_ref.shape[1], osample_ref.shape[2]
    base = samples + width
    ocolor_ref[...] = color_ref[...]
    oray_ref[...] = ray_ref[...]
    obrick_ref[0, :, :] = brick_ref[...]
    osample_ref[0, :, :] = pay_ref[0:samples, :]
    owh_ref[0, :, :] = pay_ref[samples:base, :]
    owo_ref[0, :, :] = pay_ref[base : base + 4, :]
    obh_ref[...] = pay_ref[base + 4 : base + 5, :]
    obo_ref[...] = pay_ref[base + 5 : base + 6, 0:4]


def body(ray_code, direction, target, brick_code, sample_code, w_hidden, b_hidden, w_out, b_out, brick_ids, occupancy):
    ns = lax.axis_size("slab")
    nr = lax.axis_size("ray")
    width = ray_code.shape[1]
    rays = direction.shape[0]
    slots = brick_ids.shape[1]
    bricks = brick_code.shape[1]
    samples = sample_code.shape[1]
    positions = slots * samples
    own = rays // ns
    share = bricks // nr
    part = width // nr
    early = samples // 2
    late = samples // 2 + 16
    rows_pay = samples + width + 8
    vm = pl.BlockSpec(memory_space=pltpu.VMEM)
    anywhere = pl.BlockSpec(memory_space=pl.ANY)
    sem = pltpu.SemaphoreType.DMA
    shape = jax.ShapeDtypeStruct
    vmem = pltpu.VMEM
    ins = (direction[None, :], target, brick_code[0], sample_code[0], w_hidden[0], b_hidden, w_out[0], b_out,
           brick_ids[0], occupancy)
    mid = pl.pallas_call(
        functools.partial(step_kernel, ns, nr),
        out_shape=(
            shape((3, own), f32), shape((own, width), f32), shape((share, width), f32), shape((rows_pay, width), f32),
        ),
        in_specs=[vm] + [anywhere] * len(ins),
        out_specs=(vm,) * 4,
        scratch_shapes=[vmem(v.shape, v.dtype) for v in ins] + [
            vmem((rays, width), bf16),
            vmem((slots * rays, width), bf16),
            vmem((bricks, slots * rays), bf16),
            vmem((width, samples * 128), bf16),
            vmem((width, bricks), bf16),
            vmem((width, samples), bf16),
            vmem((slots, width, rays), bf16),
            vmem((slots * rays, width), f32),
            vmem((samples, width), f32),
            vmem((4, samples, 128), f32),
            vmem((32, 8 * width), bf16),
            vmem((4, positions, rays), f32),
            vmem((positions, rays), f32),
            vmem((positions, rays), f32),
            vmem((4, rays), f32),
            vmem((ns, 4, rays), f32),
            vmem((7, positions, rays), f32),
            vmem((slots * rays // 128, 4 * samples, 128), f32),
            vmem((8 * rays, positions), f32),
            vmem((slots, 8 * rays, width), f32),
            vmem((4 * samples, width), f32),
            vmem((slots * rays, width), f32),
            vmem((rays, width), bf16),
            vmem((bricks, width), bf16),
            vmem((width, width), f32),
            vmem((late, width), bf16),
            vmem((early, width), bf16),
            vmem((ns, own, width), bf16),
            vmem((nr, share, width), bf16),
            vmem((nr, part, width), f32),
            vmem((part, width), f32),
            vmem((width, width), f32),
            vmem((nr, late, width), bf16),
            vmem((nr, early, width), bf16),
            sem((len(ins),)), sem, sem, sem, sem, sem, sem, sem, sem, sem, sem, sem, sem, sem, sem, sem, sem,
        ],
        compiler_params=pltpu.CompilerParams(
            collective_id=0, has_side_effects=True, vmem_limit_bytes=56 * 1024 * 1024
        ),
    )(ray_code, *ins)
    return pl.pallas_call(
        finish_kernel,
        out_shape=(
            shape((3, own), f32), shape((own, width), f32), shape((1, share, width), f32),
            shape((1, samples, width), f32), shape((1, width, width), f32), shape((1, width), f32),
            shape((1, 4, width), f32), shape((1, 4), f32),
        ),
        in_specs=[vm] * 4,
        out_specs=(vm,) * 8,
    )(*mid)


def solution(mesh):
    in_specs = (
        P(("ray", "slab"), None),
        P("ray"),
        P(None, "ray"),
        P("slab", None, None),
        P("slab", None, None),
        P("slab", None, None),
        P("slab", None),
        P("slab", None, None),
        P("slab", None),
        P("slab", None, "ray"),
        P("slab", "ray"),
    )
    out_specs = (
        P(None, ("ray", "slab")),
        P(("ray", "slab"), None),
        P("slab", "ray", None),
        P("slab", None, None),
        P("slab", None, None),
        P("slab", None),
        P("slab", None, None),
        P("slab", None),
    )
    return jax.shard_map(body, mesh=mesh, in_specs=in_specs, out_specs=out_specs, check_vma=False)
```

```python
import functools
import jax
import jax.numpy as jnp
from jax import lax
from jax.experimental import pallas as pl
from jax.experimental.pallas import tpu as pltpu
from jax.sharding import PartitionSpec as P

step_length = 0.002
f32 = jnp.float32
bf16 = jnp.bfloat16
MESH = pl.DeviceIdType.MESH


def mm(a, b):
    return lax.dot_general(a, b, (((1,), (0,)), ((), ())), preferred_element_type=f32)


def mt(a, b):
    return lax.dot_general(a, b, (((1,), (1,)), ((), ())), preferred_element_type=f32)


def split(x):
    hi = x.astype(bf16)
    return hi, (x - hi.astype(f32)).astype(bf16)


def mm_left(a, x):
    hi, lo = split(x)
    return mm(a, hi) + mm(a, lo)


def mt_right(x, b):
    hi, lo = split(x)
    return mt(hi, b) + mt(lo, b)


def triangle(n, strict_lower):
    row = lax.broadcasted_iota(jnp.int32, (n, n), 0)
    col = lax.broadcasted_iota(jnp.int32, (n, n), 1)
    keep = (row > col) if strict_lower else (row < col)
    return jnp.where(keep, 1.0, 0.0).astype(bf16)


def log1p_small(e):
    series = e * (1.0 - e * (0.5 - e * (1.0 / 3.0 - e * 0.25)))
    return jnp.where(e < 0.01, series, jnp.log(1.0 + e))


def one_minus_exp(o):
    series = o * (1.0 - o * (0.5 - o * (1.0 / 6.0 - o * (1.0 / 24.0))))
    return jnp.where(o < 0.03, series, 1.0 - jnp.exp(-o))


def sigmoid(x):
    return 0.5 * jnp.tanh(0.5 * x) + 0.5


def occupied_mask(occ, samples, positions):
    slot = lax.broadcasted_iota(jnp.int32, (positions, occ.shape[1]), 0) // samples
    return jnp.where(slot < occ, 1.0, 0.0)


def optical_of(raw0, occupied):
    soft = jnp.maximum(raw0, 0.0) + log1p_small(jnp.exp(-jnp.abs(raw0)))
    return step_length * soft * occupied


def torus_offsets(n):
    rows, cols = (4, n // 4) if n % 4 == 0 and n > 8 else (1, n)
    offsets = [(dr, dc) for dr in range(rows) for dc in range(cols) if (dr, dc) != (0, 0)]
    offsets.sort(key=lambda o: -(min(o[0], rows - o[0]) + min(o[1], cols - o[1])))
    return rows, cols, offsets


def peers_of(name, n):
    me = lax.axis_index(name)
    rows, cols, offsets = torus_offsets(n)
    row, col = me // cols, lax.rem(me, cols)
    return [lax.rem(row + dr, rows) * cols + lax.rem(col + dc, cols) for dr, dc in offsets]


def signal_peers(axes):
    barrier = pltpu.get_barrier_semaphore()
    for name, n in axes:
        for peer in peers_of(name, n):
            pl.semaphore_signal(barrier, inc=1, device_id={name: peer}, device_id_type=MESH)


def await_peers(axes):
    pl.semaphore_wait(pltpu.get_barrier_semaphore(), sum(n - 1 for _, n in axes))


class Exchange:
    def __init__(self, name, n, src_of, dst_of, all_of, send, recv):
        self.name, self.n, self.src_of, self.dst_of, self.all_of = name, n, src_of, dst_of, all_of
        self.send, self.recv = send, recv
        self.me = lax.axis_index(name)

    def start(self):
        for peer in peers_of(self.name, self.n):
            pltpu.make_async_remote_copy(
                src_ref=self.src_of(peer), dst_ref=self.dst_of(self.me), send_sem=self.send, recv_sem=self.recv,
                device_id={self.name: peer}, device_id_type=MESH,
            ).start()

    def wait_recv(self):
        pltpu.make_async_copy(self.all_of(self.n - 1), self.all_of(self.n - 1), self.recv).wait()

    def wait_send(self):
        pltpu.make_async_copy(self.all_of(self.n - 1), self.all_of(self.n - 1), self.send).wait()


def step_kernel(ns, nr, x_ref, dir_hbm, target_hbm, brick_hbm, sample_hbm, w_hbm, bh_hbm, wo_hbm, bo_hbm, ids_hbm,
                occ_hbm,
                color_ref, oray_ref, obrick_ref, opay_ref,
                dir_ref, target_ref, brick_ref, sample_ref, w_ref, bh_ref, wo_ref, bo_ref, ids_ref, occ_ref,
                ray_ref, xg_ref, hot_ref, wide_ref, bt_ref, st_ref, rt_ref, abt_ref, a_ref, nb_ref, corr_ref, left_ref, raw_ref, weight_ref, trail_ref,
                seg_ref, allseg_ref, basis_ref, gj_ref, gr_ref, s_ref, t_ref, ga_ref, gray_ref, gbrick_ref, pay_ref,
                late_ref, early_ref, rbuf, bbuf, pbuf, psum, pall, lbuf, ebuf,
                in_sem, xs_send, xs_recv, ss_send, ss_recv, rs_send, rs_recv, bs_send, bs_recv, ps_send, ps_recv,
                ag_send, ag_recv, ls_send, ls_recv, es_send, es_recv):
    slots, rays = ids_ref.shape
    bricks, width = brick_ref.shape
    samples = sample_ref.shape[0]
    positions = slots * samples
    own = rays // ns
    share = bricks // nr
    part = psum.shape[0]
    me = lax.axis_index("slab")
    me_r = lax.axis_index("ray")
    axes = [("slab", ns), ("ray", nr)]

    signal_peers(axes)
    loads = [
        pltpu.make_async_copy(src, dst, in_sem.at[i])
        for i, (src, dst) in enumerate([
            (w_hbm, w_ref), (sample_hbm, sample_ref), (wo_hbm, wo_ref), (bo_hbm, bo_ref), (ids_hbm, ids_ref),
            (brick_hbm, brick_ref), (bh_hbm, bh_ref), (occ_hbm, occ_ref), (dir_hbm, dir_ref),
            (target_hbm, target_ref),
        ])
    ]
    for load in loads:
        load.start()

    def rows(ref, index, size):
        return ref.at[pl.ds(pl.multiple_of(index * size, 8), size), :]

    def first(ref, size):
        return lambda count: ref.at[pl.ds(0, count * size), :]

    def lead(ref):
        return lambda count: ref.at[pl.ds(0, count)]

    x_ex = Exchange("slab", ns, lambda peer: x_ref, lambda slot: rows(ray_ref, slot, own), first(ray_ref, own),
                    xs_send, xs_recv)
    s_ex = Exchange("slab", ns, lambda peer: seg_ref, lambda slot: allseg_ref.at[slot], lead(allseg_ref),
                    ss_send, ss_recv)
    r_ex = Exchange("slab", ns, lambda peer: rows(gray_ref, peer, own), lambda slot: rbuf.at[slot], lead(rbuf),
                    rs_send, rs_recv)
    b_ex = Exchange("ray", nr, lambda peer: rows(gbrick_ref, peer, share), lambda slot: bbuf.at[slot], lead(bbuf),
                    bs_send, bs_recv)
    p_ex = Exchange("ray", nr, lambda peer: rows(pay_ref, peer, part), lambda slot: pbuf.at[slot], lead(pbuf),
                    ps_send, ps_recv)
    a_ex = Exchange("ray", nr, lambda peer: psum, lambda slot: rows(pall, slot, part), first(pall, part),
                    ag_send, ag_recv)
    l_ex = Exchange("ray", nr, lambda peer: late_ref, lambda slot: lbuf.at[slot], lead(lbuf), ls_send, ls_recv)
    e_ex = Exchange("ray", nr, lambda peer: early_ref, lambda slot: ebuf.at[slot], lead(ebuf), es_send, es_recv)

    await_peers(axes)
    x_ex.start()
    ray_ref[pl.ds(pl.multiple_of(me * own, 8), own), :] = x_ref[...]
    for load in loads[:4]:
        load.wait()
    w = w_ref[...]
    w2 = jnp.concatenate([w, w], axis=0)
    nb = -mm(sample_ref[...], w)
    nb_ref[...] = nb
    nbr = nb.astype(bf16).astype(f32)
    wo = wo_ref[...].astype(f32)
    row32 = lax.broadcasted_iota(jnp.int32, (32, width), 0) % 8
    wexp = jnp.concatenate([jnp.broadcast_to(wo[c : c + 1, :], (8, width)) for c in range(4)], axis=0)
    for q in range(8):
        left_ref[:, q * width : (q + 1) * width] = jnp.where(row32 == q, wexp, 0.0).astype(bf16)
    for c in range(4):
        corr_ref[c, :, :] = jnp.broadcast_to(
            bo_ref[0:1, c : c + 1] - jnp.sum(nbr * wo[c : c + 1, :], axis=1, keepdims=True), (samples, 128)
        )
    for load in loads[4:]:
        load.wait()
    nbt = nb.T.astype(bf16)
    pick = lax.broadcasted_iota(jnp.int32, (samples, 256), 0)
    side = lax.broadcasted_iota(jnp.int32, (samples, 256), 1) // 128
    for j in range(0, samples, 2):
        wide_ref[:, j * 128 : (j + 2) * 128] = mm(
            nbt, jnp.where(pick == side + j, 1.0, 0.0).astype(bf16)
        ).astype(bf16)
    w_twice = jnp.concatenate([w, w], axis=1)
    wt = jnp.concatenate([w.astype(f32).T.astype(bf16)] * 2, axis=1)
    bias = jnp.broadcast_to(bh_ref[...], (128, width)).T
    bias = jnp.concatenate([bias] * (rays // 128), axis=1)
    bt_ref[...] = brick_ref[...].astype(f32).T.astype(bf16)
    st_ref[...] = sample_ref[...].astype(f32).T.astype(bf16)
    lane = lax.broadcasted_iota(jnp.int32, (128, bricks), 1)
    for k in range(slots):
        for i in range(rays // 128):
            row = ids_ref[k : k + 1, i * 128 : (i + 1) * 128]
            col = jnp.broadcast_to(row, (128, 128)).T
            wide = jnp.concatenate([col] * (bricks // 128), axis=1)
            hot = jnp.where(wide == lane, 1.0, 0.0).astype(bf16)
            at = k * rays + i * 128
            xg_ref[at : at + 128, :] = mm(hot, brick_ref[...]).astype(bf16)
    for bt in range(bricks // 128):
        sub = lax.broadcasted_iota(jnp.int32, (128, rays), 0) + bt * 128
        for k in range(slots):
            hot_ref[bt * 128 : (bt + 1) * 128, k * rays : (k + 1) * rays] = jnp.where(
                ids_ref[k : k + 1, :] == sub, 1.0, 0.0
            ).astype(bf16)
    x_ex.wait_recv()

    rt_ref[...] = ray_ref[...].astype(f32).T.astype(bf16)
    for k in range(slots):
        at = k * rays
        both = jnp.concatenate([xg_ref[at : at + rays, :], ray_ref[...]], axis=1)
        a = mm(both, w2) + bh_ref[...]
        a_ref[at : at + rays, :] = a
        abt_ref[k, :, :] = (mt(wt, both) + bias).astype(bf16)

    def group(g, carry):
        k = g // (samples // 8)
        j0 = pl.multiple_of((g % (samples // 8)) * 8, 8)
        p0 = pl.multiple_of(g * 8, 8)
        fixes = [corr_ref[c, pl.ds(j0, 8), :] for c in range(4)]
        for rc in range(rays // 256):
            ab = abt_ref[k, :, rc * 256 : (rc + 1) * 256]
            acc = jnp.zeros((32, 256), f32)
            for q in range(0, 8, 2):
                parts = []
                for d in range(2):
                    n = wide_ref[:, pl.ds(pl.multiple_of((j0 + q + d) * 128, 128), 128)]
                    parts.append(jnp.maximum(ab, jnp.concatenate([n, n], axis=1)))
                acc = acc + mm(left_ref[:, q * width : (q + 2) * width], jnp.concatenate(parts, axis=0))
            for c in range(4):
                raw_ref[c, pl.ds(p0, 8), rc * 256 : (rc + 1) * 256] = acc[c * 8 : (c + 1) * 8, :] + jnp.concatenate(
                    [fixes[c], fixes[c]], axis=1
                )
        return carry

    lax.fori_loop(0, slots * samples // 8, group, 0, unroll=2)

    below = triangle(positions, True)
    above = triangle(positions, False)
    for rc in range(rays // 128):
        cols = slice(rc * 128, (rc + 1) * 128)
        raw0 = raw_ref[0, :, cols]
        occupied = occupied_mask(occ_ref[:, cols], samples, positions)
        optical = optical_of(raw0, occupied)
        entered = mm_left(below, optical)
        weight = jnp.exp(-entered) * one_minus_exp(optical)
        weight_ref[:, cols] = weight
        trail_ref[:, cols] = jnp.exp(-(entered + optical))
        basis_ref[3, :, cols] = step_length * occupied * sigmoid(raw0)
        seg = []
        for c in range(3):
            shade = sigmoid(raw_ref[c + 1, :, cols])
            raw_ref[c + 1, :, cols] = shade
            seg.append(jnp.sum(weight * shade, axis=0, keepdims=True))
        seg.append(jnp.exp(-jnp.sum(optical, axis=0, keepdims=True)))
        seg = jnp.concatenate(seg, axis=0)
        seg_ref[:, cols] = seg
        allseg_ref[me, :, cols] = seg
    s_ex.start()

    col_sums = []
    all_levels = []
    ends = []
    for rc in range(rays // 128):
        cols = slice(rc * 128, (rc + 1) * 128)
        weight = weight_ref[:, cols]
        trail = trail_ref[:, cols]
        dens = basis_ref[3, :, cols]
        lit = [weight * raw_ref[c + 1, :, cols] for c in range(3)]
        after = mm_left(above, jnp.concatenate(lit, axis=1))
        base = rc * 128 * 8
        levels = []
        parts = []
        for c in range(3):
            shade = raw_ref[c + 1, :, cols]
            u = shade * trail - after[:, c * 128 : (c + 1) * 128]
            level = jnp.mean(u, axis=0, keepdims=True)
            levels.append(level)
            u = dens * (u - level)
            y = lit[c] * (1.0 - shade)
            basis_ref[c, :, cols] = u
            basis_ref[4 + c, :, cols] = y
            parts.append((c, u))
            parts.append((4 + c, y))
        parts.append((3, dens))
        sums = [None] * 7
        for b, value in parts:
            gr_ref[pl.ds(base + b, 128, stride=8), :] = value.T
            sums[b] = jnp.sum(value, axis=0, keepdims=True)
        gr_ref[pl.ds(base + 7, 128, stride=8), :] = jnp.zeros((128, positions), f32)
        col_sums.append(sums)
        all_levels.append(levels)

    lane_p = lax.broadcasted_iota(jnp.int32, (16, positions), 1)

    def ray_group(rg, carry):
        r0 = pl.multiple_of(rg * 8, 8)
        a0 = a_ref[pl.ds(r0, 8), :]
        a1 = a_ref[pl.ds(rays + r0, 8), :]
        for i in range(0, 8, 2):
            halves = []
            for r in (i, i + 1):
                m0 = jnp.where(a0[r : r + 1, :] > nb, 1.0, 0.0).astype(bf16)
                m1 = jnp.where(a1[r : r + 1, :] > nb, 1.0, 0.0).astype(bf16)
                halves.append(jnp.concatenate([m0, m1], axis=0))
            m = jnp.concatenate(halves, axis=1)
            at = pl.multiple_of((r0 + i) * 8, 16)
            g16 = gr_ref[pl.ds(at, 16), :]
            left = jnp.concatenate(
                [jnp.where(lane_p < samples, g16, 0.0), jnp.where(lane_p < samples, 0.0, g16)], axis=0
            ).astype(bf16)
            out = mm(left, m)
            for k in range(2):
                s_ref[k, pl.ds(at, 8), :] = out[k * 16 : k * 16 + 8, :width]
                s_ref[k, pl.ds(pl.multiple_of(at + 8, 8), 8), :] = out[k * 16 + 8 : k * 16 + 16, width:]
        return carry

    lax.fori_loop(0, rays // 8, ray_group, 0, unroll=4)

    s_ex.wait_recv()
    zero3 = jnp.zeros((3, rays), f32)
    one1 = jnp.ones((1, rays), f32)
    ahead = dir_ref[...] == 0

    def low_step(t, state):
        color, trans = state
        piece, through = allseg_ref[t, 0:3, :], allseg_ref[t, 3:4, :]
        color = jnp.where(ahead, color + trans * piece, piece + through * color)
        return color, trans * through

    def high_step(i, state):
        t = ns - 1 - i
        color, trans = state
        piece, through = allseg_ref[t, 0:3, :], allseg_ref[t, 3:4, :]
        color = jnp.where(ahead, piece + through * color, color + trans * piece)
        return color, trans * through

    low_c, low_t = lax.fori_loop(0, me, low_step, (zero3, one1))
    high_c, high_t = lax.fori_loop(0, ns - 1 - me, high_step, (zero3, one1))
    seg_c, seg_t = allseg_ref[me, 0:3, :], allseg_ref[me, 3:4, :]
    before_c = jnp.where(ahead, low_c, high_c)
    before_t = jnp.where(ahead, low_t, high_t)
    after_c = jnp.where(ahead, high_c, low_c)
    color = before_c + before_t * (seg_c + seg_t * after_c)
    residual = color - target_ref[...]
    cot_c = before_t * residual
    tail = before_t * jnp.sum(after_c * residual, axis=0, keepdims=True) * seg_t
    color8 = jnp.concatenate([color, jnp.zeros((5, rays), f32)], axis=0)
    color_ref[...] = pltpu.roll(color8, lax.rem(rays - me * own, rays), 1)[0:3, 0:own]

    lane_row = lax.broadcasted_iota(jnp.int32, (1, width), 1)
    bout = jnp.zeros((1, width), f32)
    gw_out = [jnp.zeros((1, width), f32) for _ in range(4)]
    for rc in range(rays // 128):
        cols = slice(rc * 128, (rc + 1) * 128)
        cots = [cot_c[c : c + 1, cols] for c in range(3)]
        end = tail[:, cols]
        for c in range(3):
            end = end - cots[c] * all_levels[rc][c]
        ends.append(end)
        sums = col_sums[rc]
        total0 = cots[0] * sums[0] + cots[1] * sums[1] + cots[2] * sums[2] - end * sums[3]
        bout = bout + jnp.where(lane_row == 0, jnp.sum(total0), 0.0)
        for c in range(3):
            bout = bout + jnp.where(lane_row == c + 1, jnp.sum(cots[c] * sums[4 + c]), 0.0)
        wide = [jnp.broadcast_to(v, (128, 128)).T for v in cots + [end]]
        for k in range(slots):
            take = lambda b: s_ref[k, pl.ds(rc * 1024 + b, 128, stride=8), :]
            s_all = [wide[0] * take(0) + wide[1] * take(1) + wide[2] * take(2) - wide[3] * take(3)]
            s_all += [wide[c] * take(4 + c) for c in range(3)]
            at = k * rays + rc * 128
            a = a_ref[at : at + 128, :]
            ga = jnp.zeros((128, width), f32)
            for c in range(4):
                ga = ga + s_all[c] * wo[c : c + 1, :]
                gw_out[c] = gw_out[c] + jnp.sum(s_all[c] * a, axis=0, keepdims=True)
            ga_ref[at : at + 128, :] = ga
    ga_sum = ga_ref[0:rays, :] + ga_ref[rays:, :]
    gray_ref[...] = mt(jnp.concatenate(split(ga_sum), axis=1), w_twice).astype(bf16)
    r_ex.start()
    rbuf[me, :, :] = gray_ref[pl.ds(pl.multiple_of(me * own, 8), own), :]

    pre = mm(hot_ref[...], ga_ref[...].astype(bf16))
    pre_hi, pre_lo = split(pre)
    gbrick_ref[...] = mt(jnp.concatenate([pre_hi, pre_lo], axis=1), w_twice).astype(bf16)
    b_ex.start()
    bbuf[me_r, :, :] = gbrick_ref[pl.ds(pl.multiple_of(me_r * share, 8), share), :]

    pay_ref[...] = mm(bt_ref[...], pre_hi) + mm(rt_ref[...], ga_sum.astype(bf16))
    p_ex.start()
    pbuf[me_r, :, :] = pay_ref[pl.ds(pl.multiple_of(me_r * part, 8), part), :]

    for rc in range(rays // 128):
        cols = slice(rc * 128, (rc + 1) * 128)
        cots = [cot_c[c : c + 1, cols] for c in range(3)]
        grads = [-ends[rc] * basis_ref[3, :, cols]]
        for c in range(3):
            grads[0] = grads[0] + cots[c] * basis_ref[c, :, cols]
            grads.append(cots[c] * basis_ref[4 + c, :, cols])
        for c in range(4):
            for k in range(slots):
                gj_ref[k * (rays // 128) + rc, pl.ds(c, samples, stride=4), :] = grads[c][
                    k * samples : (k + 1) * samples, :
                ]

    sub8 = lax.broadcasted_iota(jnp.int32, (8, width), 0)

    def sample_pair(jp, carry):
        row8 = pl.multiple_of(jp * 8, 8)
        n0 = nb_ref[pl.ds(jp * 2, 1), :]
        n1 = nb_ref[pl.ds(jp * 2 + 1, 1), :]
        acc = jnp.zeros((8, 2 * width), f32)
        for i in range(slots * rays // 256):
            a = a_ref[i * 256 : (i + 1) * 256, :]
            m = jnp.concatenate(
                [jnp.where(a > n0, 1.0, 0.0).astype(bf16), jnp.where(a > n1, 1.0, 0.0).astype(bf16)], axis=1
            )
            left = jnp.concatenate([gj_ref[2 * i, pl.ds(row8, 8), :], gj_ref[2 * i + 1, pl.ds(row8, 8), :]], axis=1)
            acc = acc + mm(left.astype(bf16), m)
        t_ref[pl.ds(row8, 8), :] = jnp.where(sub8 < 4, acc[:, :width], acc[:, width:])
        return carry

    gb_sum = jnp.zeros((1, width), f32)
    mid = samples // 2
    for h in range(2):
        lax.fori_loop(h * mid // 2, (h + 1) * mid // 2, sample_pair, 0, unroll=4)
        gb = jnp.zeros((mid, width), f32)
        for c in range(4):
            t_c = t_ref[pl.ds(h * mid * 4 + c, mid, stride=4), :]
            gb = gb + t_c * wo[c : c + 1, :]
            gw_out[c] = gw_out[c] - jnp.sum(t_c * nb[h * mid : (h + 1) * mid, :], axis=0, keepdims=True)
        gb_sum = gb_sum + jnp.sum(gb, axis=0, keepdims=True)
        if h == 0:
            early_ref[...] = gb.astype(bf16)
            e_ex.start()
            ebuf[me_r, :, :] = early_ref[...]
        else:
            small = jnp.concatenate(gw_out + [gb_sum, bout, jnp.zeros((2, width), f32)], axis=0)
            late_ref[...] = jnp.concatenate([gb.astype(bf16)] + [v for v in split(small)], axis=0)
            l_ex.start()
            lbuf[me_r, :, :] = late_ref[...]
    p_ex.wait_recv()
    total = pbuf[0, :, :]
    for i in range(1, nr):
        total = total + pbuf[i, :, :]
    psum[...] = total
    pall[pl.ds(pl.multiple_of(me_r * part, 8), part), :] = total
    a_ex.start()
    b_ex.wait_recv()
    total = bbuf[0, :, :].astype(f32)
    for i in range(1, nr):
        total = total + bbuf[i, :, :].astype(f32)
    obrick_ref[...] = total
    r_ex.wait_recv()
    total = rbuf[0, :, :].astype(f32)
    for i in range(1, ns):
        total = total + rbuf[i, :, :].astype(f32)
    oray_ref[...] = total
    x_ex.wait_send()
    s_ex.wait_send()
    r_ex.wait_send()
    b_ex.wait_send()
    p_ex.wait_send()
    e_ex.wait_recv()
    l_ex.wait_recv()
    front = ebuf[0, :, :].astype(f32)
    total = lbuf[0, :, :].astype(f32)
    for i in range(1, nr):
        front = front + ebuf[i, :, :].astype(f32)
        total = total + lbuf[i, :, :].astype(f32)
    gb = jnp.concatenate([front, total[0:mid, :]], axis=0)
    opay_ref[0:samples, :] = mt_right(gb, w)
    opay_ref[samples + width :, :] = total[mid : mid + 8, :] + total[mid + 8 :, :]
    extra = mm_left(st_ref[...], gb)
    a_ex.wait_recv()
    opay_ref[samples : samples + width, :] = pall[...] + extra
    a_ex.wait_send()
    e_ex.wait_send()
    l_ex.wait_send()


def finish_kernel(color_ref, ray_ref, brick_ref, pay_ref,
                  ocolor_ref, oray_ref, obrick_ref, osample_ref, owh_ref, obh_ref, owo_ref, obo_ref):
    samples, width = osample_ref.shape[1], osample_ref.shape[2]
    base = samples + width
    ocolor_ref[...] = color_ref[...]
    oray_ref[...] = ray_ref[...]
    obrick_ref[0, :, :] = brick_ref[...]
    osample_ref[0, :, :] = pay_ref[0:samples, :]
    owh_ref[0, :, :] = pay_ref[samples:base, :]
    owo_ref[0, :, :] = pay_ref[base : base + 4, :]
    obh_ref[...] = pay_ref[base + 4 : base + 5, :]
    obo_ref[...] = pay_ref[base + 5 : base + 6, 0:4]


def body(ray_code, direction, target, brick_code, sample_code, w_hidden, b_hidden, w_out, b_out, brick_ids, occupancy):
    ns = lax.axis_size("slab")
    nr = lax.axis_size("ray")
    width = ray_code.shape[1]
    rays = direction.shape[0]
    slots = brick_ids.shape[1]
    bricks = brick_code.shape[1]
    samples = sample_code.shape[1]
    positions = slots * samples
    own = rays // ns
    share = bricks // nr
    part = width // nr
    early = samples // 2
    late = samples // 2 + 16
    rows_pay = samples + width + 8
    vm = pl.BlockSpec(memory_space=pltpu.VMEM)
    anywhere = pl.BlockSpec(memory_space=pl.ANY)
    sem = pltpu.SemaphoreType.DMA
    shape = jax.ShapeDtypeStruct
    vmem = pltpu.VMEM
    ins = (direction[None, :], target, brick_code[0], sample_code[0], w_hidden[0], b_hidden, w_out[0], b_out,
           brick_ids[0], occupancy)
    mid = pl.pallas_call(
        functools.partial(step_kernel, ns, nr),
        out_shape=(
            shape((3, own), f32), shape((own, width), f32), shape((share, width), f32), shape((rows_pay, width), f32),
        ),
        in_specs=[vm] + [anywhere] * len(ins),
        out_specs=(vm,) * 4,
        scratch_shapes=[vmem(v.shape, v.dtype) for v in ins] + [
            vmem((rays, width), bf16),
            vmem((slots * rays, width), bf16),
            vmem((bricks, slots * rays), bf16),
            vmem((width, samples * 128), bf16),
            vmem((width, bricks), bf16),
            vmem((width, samples), bf16),
            vmem((width, rays), bf16),
            vmem((slots, width, rays), bf16),
            vmem((slots * rays, width), f32),
            vmem((samples, width), f32),
            vmem((4, samples, 128), f32),
            vmem((32, 8 * width), bf16),
            vmem((4, positions, rays), f32),
            vmem((positions, rays), f32),
            vmem((positions, rays), f32),
            vmem((4, rays), f32),
            vmem((ns, 4, rays), f32),
            vmem((7, positions, rays), f32),
            vmem((slots * rays // 128, 4 * samples, 128), f32),
            vmem((8 * rays, positions), f32),
            vmem((slots, 8 * rays, width), f32),
            vmem((4 * samples, width), f32),
            vmem((slots * rays, width), f32),
            vmem((rays, width), bf16),
            vmem((bricks, width), bf16),
            vmem((width, width), f32),
            vmem((late, width), bf16),
            vmem((early, width), bf16),
            vmem((ns, own, width), bf16),
            vmem((nr, share, width), bf16),
            vmem((nr, part, width), f32),
            vmem((part, width), f32),
            vmem((width, width), f32),
            vmem((nr, late, width), bf16),
            vmem((nr, early, width), bf16),
            sem((len(ins),)), sem, sem, sem, sem, sem, sem, sem, sem, sem, sem, sem, sem, sem, sem, sem, sem,
        ],
        compiler_params=pltpu.CompilerParams(
            collective_id=0, has_side_effects=True, vmem_limit_bytes=56 * 1024 * 1024
        ),
    )(ray_code, *ins)
    return pl.pallas_call(
        finish_kernel,
        out_shape=(
            shape((3, own), f32), shape((own, width), f32), shape((1, share, width), f32),
            shape((1, samples, width), f32), shape((1, width, width), f32), shape((1, width), f32),
            shape((1, 4, width), f32), shape((1, 4), f32),
        ),
        in_specs=[vm] * 4,
        out_specs=(vm,) * 8,
    )(*mid)


def solution(mesh):
    in_specs = (
        P(("ray", "slab"), None),
        P("ray"),
        P(None, "ray"),
        P("slab", None, None),
        P("slab", None, None),
        P("slab", None, None),
        P("slab", None),
        P("slab", None, None),
        P("slab", None),
        P("slab", None, "ray"),
        P("slab", "ray"),
    )
    out_specs = (
        P(None, ("ray", "slab")),
        P(("ray", "slab"), None),
        P("slab", "ray", None),
        P("slab", None, None),
        P("slab", None, None),
        P("slab", None),
        P("slab", None, None),
        P("slab", None),
    )
    return jax.shard_map(body, mesh=mesh, in_specs=in_specs, out_specs=out_specs, check_vma=False)
```
